512 devices in a mesh: tile: 32 (over z, y_lo, core), scan: 16 (over x, y_hi).
Axes of the slice: x: 4, y: 8 (y_hi: 4, y_lo: 2; y = y_hi * 2 + y_lo), z: 8, core: 2. Of those that a mesh axis runs over, the one named last changes fastest.
Arguments:
- object_tiles: float32 [2, 384, 8192], P(None, None, 'tile'), may hold values from -6 to 6
- probe_modes: bfloat16 [2, 4, 256, 256], replicated, may hold values from -3 to 3
- amplitudes: bfloat16 [32, 16, 5, 256, 256], P('tile', 'scan'), may hold values from 0 to 3
- row_offsets: int32 [32, 16, 5], P('tile', 'scan'), may hold values from 0 to 128
- col_offsets: int32 [32, 16, 5], P('tile', 'scan'), may hold values from 0 to 255
- slot_counts: int32 [32, 16], P('tile', 'scan'), may hold values from 0 to 5, as said below
Outputs:
- new_object: float32 [2, 384, 8192], P(None, None, 'tile')
- new_probe: float32 [2, 4, 256, 256], replicated
The draws below stay inside these ranges and needn't reach their ends.
Inputs may be any that keep to these rules, and one draw needn't show every extreme that they name: `slot_counts`: in every row of tiles the counts sum to 32, and one device of each row holds 5 positions.
All inputs are finite; a program needn't handle non-finite values.
Results may differ from the reference program's by a relative error of at most 0.00075.
The reference program's roundings to bfloat16 on the way count: a program that leaves them out, or rounds other values in their place, can miss the bound.
Values may be sent and summed in bfloat16 or wider, within the bound.
A program may use at most 64 MiB of HBM per device.

```python
import math
import jax
import jax.numpy as jnp
from jax import lax

P_SIZE = 256
MODES = 4
TH = 384
TW = 256
SLOTS = 5
OBJ_COLS = 8192
N_TILE = 32
N_SCAN = 16


def draw_slot_counts(key, part):
    remain = 2 * N_SCAN - SLOTS
    base = remain // (N_SCAN - 1)
    extra = remain % (N_SCAN - 1)
    pattern = jnp.concatenate([jnp.full((1,), SLOTS, jnp.int32), jnp.full((extra,), base + 1, jnp.int32), jnp.full((N_SCAN - 1 - extra,), base, jnp.int32)])
    row_keys = jax.random.split(key, N_TILE)
    return jax.vmap(lambda row_key: jax.random.permutation(row_key, pattern))(row_keys)


def place_ends(drawn, key, smallest, largest):
    longest = drawn.shape.index(max(drawn.shape))
    spots = []
    for shift in (0, 1):
        where = [jax.random.randint(jax.random.fold_in(key, axis), (), 0, length) for axis, length in enumerate(drawn.shape)]
        where[longest] = (where[longest] + shift) % drawn.shape[longest]
        spots.append(tuple(where))
    return drawn.at[spots[0]].set(smallest).at[spots[1]].set(largest)


def block_levels(stream_key, dims, cuts, low, top_value):
    level, own = 1.0, jax.random.fold_in(stream_key, 6)
    for position, shards_of in cuts:
        draws = jnp.exp(jax.random.uniform(jax.random.fold_in(own, position), (shards_of,), jnp.float32, low / len(cuts), top_value / len(cuts)))
        level = level * jnp.repeat(draws, dims[position] // shards_of).reshape([-1 if axis == position else 1 for axis in range(len(dims))])
    return level


def bell_draw(rng, shape, scale, bound, pieces=(), kind=jnp.bfloat16):
    array = scale * jax.random.normal(rng, shape, jnp.float32)
    if pieces:
        array = array * block_levels(rng, shape, pieces, -0.22, 0.18)
    return jnp.clip(array, -bound, bound).astype(kind)


def setup_inputs(seed: int = 0) -> dict:
    splits = jax.random.split(jax.random.key(seed), 7)
    object_tiles = bell_draw(splits[0], (2, TH, OBJ_COLS), 1.0, 6.0, ((2, 32),), jnp.float32)
    probe_modes = bell_draw(splits[1], (2, MODES, P_SIZE, P_SIZE), 0.5, 3.0)
    amplitudes = jnp.clip(3.0 * jax.random.uniform(splits[2], (N_TILE, N_SCAN, SLOTS, P_SIZE, P_SIZE), jnp.float32) ** block_levels(splits[2], (N_TILE, N_SCAN, SLOTS, P_SIZE, P_SIZE), ((0, 32), (1, 16)), -0.2, 0.2), 0.0, 3.0).astype(jnp.bfloat16)
    row_offsets = place_ends(jax.random.randint(splits[3], (N_TILE, N_SCAN, SLOTS), 0, TH - P_SIZE + 1), jax.random.fold_in(splits[3], 1), 0, TH - P_SIZE).astype(jnp.int32)
    col_offsets = place_ends(jax.random.randint(splits[4], (N_TILE, N_SCAN, SLOTS), 0, TW), jax.random.fold_in(splits[4], 1), 0, TW - 1).astype(jnp.int32)
    slot_counts = draw_slot_counts(jax.random.fold_in(splits[6], 71), 0)
    return {"object_tiles": object_tiles, "probe_modes": probe_modes, "amplitudes": amplitudes, "row_offsets": row_offsets, "col_offsets": col_offsets, "slot_counts": slot_counts}


object_step = 0.1
probe_scale = 0.5

def dft_tables(extent):
    index = jnp.arange(extent, dtype=jnp.int32)
    phase = index[:, None] * index[None, :] % extent
    angle = phase.astype(jnp.float32) * (2.0 * math.pi / extent)
    factor = 1.0 / math.sqrt(extent)
    return ((jnp.cos(angle) * factor).astype(jnp.bfloat16), (-jnp.sin(angle) * factor).astype(jnp.bfloat16))

def left_apply(mat_real, mat_imag, val_real, val_imag):
    a_mat = mat_real.astype(jnp.float32)
    b_mat = mat_imag.astype(jnp.float32)
    u_val = val_real.astype(jnp.float32)
    v_val = val_imag.astype(jnp.float32)
    out_real = jnp.einsum('kl,mlj->mkj', a_mat, u_val) - jnp.einsum('kl,mlj->mkj', b_mat, v_val)
    out_imag = jnp.einsum('kl,mlj->mkj', a_mat, v_val) + jnp.einsum('kl,mlj->mkj', b_mat, u_val)
    return (out_real, out_imag)

def right_apply(val_real, val_imag, mat_real, mat_imag):
    a_mat = mat_real.astype(jnp.float32)
    b_mat = mat_imag.astype(jnp.float32)
    u_val = val_real.astype(jnp.float32)
    v_val = val_imag.astype(jnp.float32)
    out_real = jnp.einsum('mkl,lj->mkj', u_val, a_mat) - jnp.einsum('mkl,lj->mkj', v_val, b_mat)
    out_imag = jnp.einsum('mkl,lj->mkj', v_val, a_mat) + jnp.einsum('mkl,lj->mkj', u_val, b_mat)
    return (out_real, out_imag)

def position_terms(prb_real, prb_imag, patch_real, patch_imag, amplitude, dft_real, dft_imag):
    psi_real = (prb_real * patch_real - prb_imag * patch_imag).astype(jnp.bfloat16)
    psi_imag = (prb_real * patch_imag + prb_imag * patch_real).astype(jnp.bfloat16)
    a_real, a_imag = left_apply(dft_real, dft_imag, psi_real, psi_imag)
    f_real, f_imag = right_apply(a_real.astype(jnp.bfloat16), a_imag.astype(jnp.bfloat16), dft_real, dft_imag)
    intensity = lax.optimization_barrier(jnp.sum(f_real * f_real + f_imag * f_imag, axis=0))
    factor = amplitude.astype(jnp.float32) / jnp.sqrt(intensity + 1.0) - 1.0
    d_real = (f_real * factor).astype(jnp.bfloat16)
    d_imag = (f_imag * factor).astype(jnp.bfloat16)
    b_real, b_imag = left_apply(dft_real, -dft_imag, d_real, d_imag)
    e_real, e_imag = right_apply(b_real.astype(jnp.bfloat16), b_imag.astype(jnp.bfloat16), dft_real, -dft_imag)
    obj_real = lax.optimization_barrier(jnp.sum(prb_real * e_real + prb_imag * e_imag, axis=0))
    obj_imag = lax.optimization_barrier(jnp.sum(prb_real * e_imag - prb_imag * e_real, axis=0))
    grad_real = patch_real * e_real + patch_imag * e_imag
    grad_imag = patch_real * e_imag - patch_imag * e_real
    return (jnp.stack([obj_real, obj_imag]), jnp.stack([grad_real, grad_imag]))

def reference(object_tiles, probe_modes, amplitudes, row_offsets, col_offsets, slot_counts):
    dft_real, dft_imag = dft_tables(P_SIZE)
    probe_f = probe_modes.astype(jnp.float32)
    padded = jnp.pad(object_tiles, ((0, 0), (0, 0), (0, TW)))
    ends_at = jnp.cumsum(slot_counts, axis=1).astype(jnp.int32)
    starts = (ends_at - slot_counts).astype(jnp.int32)
    rank_list = jnp.arange(2 * N_SCAN, dtype=jnp.int32)

    def row_step(carry, tile_at):
        source = lax.optimization_barrier(jnp.sum((ends_at[tile_at][None, :] <= rank_list[:, None]).astype(jnp.int32), axis=1)).astype(jnp.int32)
        slot_index = (rank_list - starts[tile_at][source]).astype(jnp.int32)
        amp_list = amplitudes[tile_at, source, slot_index]
        row_list = row_offsets[tile_at, source, slot_index].astype(jnp.int32)
        col_list = col_offsets[tile_at, source, slot_index].astype(jnp.int32)

        def single(inner, item):
            obj_grad, probe_grad = inner
            amplitude, row_at, col_at = item
            col_start = (tile_at * TW + col_at).astype(jnp.int32)
            zero_at = jnp.zeros((), jnp.int32)
            patch_cells = lax.dynamic_slice(padded, (zero_at, row_at, col_start), (2, P_SIZE, P_SIZE))
            obj_term, probe_term = position_terms(probe_f[0], probe_f[1], patch_cells[0], patch_cells[1], amplitude, dft_real, dft_imag)
            current = lax.dynamic_slice(obj_grad, (zero_at, row_at, col_start), (2, P_SIZE, P_SIZE))
            obj_grad = lax.dynamic_update_slice(obj_grad, current + obj_term, (zero_at, row_at, col_start))
            return ((obj_grad, probe_grad + probe_term), None)
        carry, _ = lax.scan(single, carry, (amp_list, row_list, col_list))
        return (carry, None)
    start_grad = (jnp.zeros(padded.shape, jnp.float32), jnp.zeros(probe_modes.shape, jnp.float32))
    (obj_grad, probe_grad), _ = lax.scan(row_step, start_grad, jnp.arange(N_TILE, dtype=jnp.int32))
    new_object = object_tiles + object_step * obj_grad[:, :, :TW * N_TILE]
    factor = probe_scale / math.sqrt(N_TILE * N_SCAN)
    new_probe = probe_f + factor * probe_grad
    return (new_object, new_probe)
```

```python
import functools
import math

import jax
import jax.numpy as jnp
import numpy as np
from jax import lax
from jax.experimental import pallas as pl
from jax.experimental.pallas import tpu as pltpu
from jax.sharding import PartitionSpec as P

F32, BF16 = jnp.float32, jnp.bfloat16
MESH = pl.DeviceIdType.MESH
KEEP = 2
SIZES = (8, 2, 2, 4, 4)
object_step = 0.1
probe_scale = 0.5


def dft_tables(extent):
    index = np.arange(extent)
    angle = (index[:, None] * index[None, :] % extent) * (2.0 * math.pi / extent)
    factor = 1.0 / math.sqrt(extent)
    table = np.stack([np.cos(angle) * factor, -np.sin(angle) * factor])
    return jnp.asarray(table.astype(np.float32)).astype(BF16)


def rows_loop(total, step, body):
    def trip(i, carry):
        body(pl.multiple_of(i * step, step))
        return carry
    lax.fori_loop(0, total // step, trip, 0)


def dot(a, b):
    return jnp.dot(a, b, preferred_element_type=F32)


def positions_kernel(mine, others, tile, halo, probe, amp_own, amp_got, table,
                     grad_out, prb_out,
                     amp, lanes, patch, stack, side, wide, term, forward, inverse, arrived):
    n = probe.shape[2]
    modes = probe.shape[1]
    height, tw = tile.shape[1], tile.shape[2]
    tall = n + 8
    edge = mine[3, 0] > 0

    def clear(at):
        grad_out[:, :, pl.ds(at, 8), :] = jnp.zeros((2, 2, 8, tw), F32)
    rows_loop(height, 8, clear)

    def clear_probe(at):
        prb_out[:, :, pl.ds(at, 8), :] = jnp.zeros((2, modes, 8, n), F32)
    rows_loop(n, 8, clear_probe)

    forward[:n, :n] = table[0]
    forward[n:, n:] = table[0]
    forward[n:, :n] = table[1]
    forward[:n, n:] = -table[1]
    inverse[:n, :n] = table[0]
    inverse[n:, n:] = table[0]
    inverse[n:, :n] = -table[1]
    inverse[:n, n:] = table[1]

    def position(r, c):
        base = pl.multiple_of(jnp.minimum(r // 8 * 8, height - tall), 8)
        rem = r - base
        back_r = tall - rem
        back_c = lax.rem(2 * tw - c, 2 * tw)

        def lane_in(at):
            rows = pl.ds(pl.multiple_of(base + at, 8), 24)
            for p in range(2):
                beside = jnp.where(edge, 0.0, halo[p, rows, :])
                x = jnp.concatenate([tile[p, rows, :], beside], 1)
                lanes[p, pl.ds(at, 24), :] = pltpu.roll(x, back_c, 1)[:, :n]
        rows_loop(tall, 24, lane_in)
        for p in range(2):
            for h in range(n // 128):
                cols = pl.ds(h * 128, 128)
                patch[p, :, cols] = pltpu.roll(lanes[p, :, cols], back_r, 0)[:n]

        def make_psi(at):
            rows, low = pl.ds(at, 16), pl.ds(pl.multiple_of(at + n, 16), 16)
            xr, xi = patch[0, rows, :], patch[1, rows, :]
            for m in range(modes):
                pr = probe[0, m, rows, :].astype(F32)
                pi = probe[1, m, rows, :].astype(F32)
                stack[m, rows, :] = (pr * xr - pi * xi).astype(BF16)
                stack[m, low, :] = (pr * xi + pi * xr).astype(BF16)
        rows_loop(n, 16, make_psi)

        for m in range(modes):
            a = dot(forward[...], stack[m]).astype(BF16)
            side[m, :, :n] = a[:n]
            side[m, :, n:] = a[n:]
        for m in range(modes):
            wide[m] = dot(side[m], inverse[...])

        pltpu.make_async_copy(amp_own.at[0], amp, arrived).wait()

        def make_d(at):
            rows, low = pl.ds(at, 16), pl.ds(pl.multiple_of(at + n, 16), 16)
            total = jnp.zeros((16, n), F32)
            for m in range(modes):
                fr, fi = wide[m, rows, :n], wide[m, rows, n:]
                total += fr * fr + fi * fi
            factor = amp[rows, :].astype(F32) / jnp.sqrt(total + 1.0) - 1.0
            for m in range(modes):
                stack[m, rows, :] = (wide[m, rows, :n] * factor).astype(BF16)
                stack[m, low, :] = (wide[m, rows, n:] * factor).astype(BF16)
        rows_loop(n, 16, make_d)

        for m in range(modes):
            b = dot(inverse[...], stack[m]).astype(BF16)
            side[m, :, :n] = b[:n]
            side[m, :, n:] = b[n:]
        for m in range(modes):
            wide[m] = dot(side[m], forward[...])

        def finish(at):
            rows = pl.ds(at, 16)
            xr, xi = patch[0, rows, :], patch[1, rows, :]
            tr = jnp.zeros((16, n), F32)
            ti = jnp.zeros((16, n), F32)
            for m in range(modes):
                er, ei = wide[m, rows, :n], wide[m, rows, n:]
                pr = probe[0, m, rows, :].astype(F32)
                pi = probe[1, m, rows, :].astype(F32)
                tr += pr * er + pi * ei
                ti += pr * ei - pi * er
                prb_out[0, m, rows, :] += xr * er + xi * ei
                prb_out[1, m, rows, :] += xr * ei - xi * er
            term[0, rows, :] = tr
            term[1, rows, :] = ti
        rows_loop(n, 16, finish)

        term[:, n:, :] = jnp.zeros((2, 8, n), F32)
        for p in range(2):
            for h in range(n // 128):
                cols = pl.ds(h * 128, 128)
                lanes[p, :, cols] = pltpu.roll(term[p, :, cols], rem, 0)

        def lane_out(at):
            rows = pl.ds(pl.multiple_of(base + at, 8), 24)
            for p in range(2):
                y = lanes[p, pl.ds(at, 24), :]
                y = pltpu.roll(jnp.concatenate([y, jnp.zeros_like(y)], 1), c, 1)
                grad_out[0, p, rows, :] += y[:, :tw]
                grad_out[1, p, rows, :] += y[:, tw:]
        rows_loop(tall, 24, lane_out)

    slots = KEEP + amp_got.shape[0]

    def item_trip(item, carry):
        own = item < KEEP
        other = jnp.maximum(item - KEEP, 0)
        r = jnp.where(own, mine[0, item], others[other, 0, item])
        c = jnp.where(own, mine[1, item], others[other, 1, item])
        count = jnp.where(own, mine[2, item], others[other, 2, item])

        @pl.when(item < count)
        def _():
            @pl.when(own)
            def _():
                pltpu.make_async_copy(amp_own.at[item], amp, arrived).start()

            @pl.when(jnp.logical_not(own))
            def _():
                pltpu.make_async_copy(amp_got.at[other], amp, arrived).start()
            position(r, c)
        return carry
    lax.fori_loop(0, slots, item_trip, 0)

    @pl.when(edge)
    def _():
        def drop(at):
            grad_out[1, :, pl.ds(at, 8), :] = jnp.zeros((2, 8, tw), F32)
        rows_loop(height, 8, drop)


def positions(mine, others, tile, halo, probe, amp_own, amp_got, table):
    _, modes, n, _ = probe.shape
    height, tw = tile.shape[1:]
    vmem, smem = pl.BlockSpec(memory_space=pltpu.VMEM), pl.BlockSpec(memory_space=pltpu.SMEM)
    anywhere = pl.BlockSpec(memory_space=pl.ANY)
    return pl.pallas_call(
        positions_kernel,
        out_shape=(
            jax.ShapeDtypeStruct((2, 2, height, tw), F32),
            jax.ShapeDtypeStruct((2, modes, n, n), F32),
        ),
        in_specs=[smem, smem, vmem, vmem, vmem, anywhere, anywhere, vmem],
        out_specs=(vmem, vmem),
        scratch_shapes=[
            pltpu.VMEM((n, n), BF16),
            pltpu.VMEM((2, n + 8, n), F32),
            pltpu.VMEM((2, n, n), F32),
            pltpu.VMEM((modes, 2 * n, n), BF16),
            pltpu.VMEM((modes, n, 2 * n), BF16),
            pltpu.VMEM((modes, n, 2 * n), F32),
            pltpu.VMEM((2, n + 8, n), F32),
            pltpu.VMEM((2 * n, 2 * n), BF16),
            pltpu.VMEM((2 * n, 2 * n), BF16),
            pltpu.SemaphoreType.DMA,
        ],
        compiler_params=pltpu.CompilerParams(vmem_limit_bytes=48 << 20),
        name="positions",
    )(mine, others, tile, halo, probe, amp_own, amp_got, table)


class Place:
    def __init__(self, sizes):
        self.nz, self.nlo, self.nc, self.nx, self.nhi = sizes
        self.ny = self.nlo * self.nhi
        self.tiles, self.scans = self.nz * self.nlo * self.nc, self.nx * self.nhi
        self.t, self.s = lax.axis_index("tile"), lax.axis_index("scan")
        self.core = lax.rem(self.t, self.nc)
        self.lo = lax.rem(self.t // self.nc, self.nlo)
        self.z = self.t // (self.nc * self.nlo)
        self.x, self.hi = self.s // self.nhi, lax.rem(self.s, self.nhi)
        self.y = self.hi * self.nlo + self.lo

    def device(self, z, y, core, x):
        lo, hi = lax.rem(y, self.nlo), y // self.nlo
        return {"tile": (z * self.nlo + lo) * self.nc + core, "scan": x * self.nhi + hi}

    def along_z(self, d):
        at = lax.rem(self.z + d, self.nz)
        return at, self.device(at, self.y, self.core, self.x)

    def along_y(self, d):
        at = lax.rem(self.y + d, self.ny)
        return at, self.device(self.z, at, self.core, self.x)

    def along_hi(self, d):
        at = lax.rem(self.hi + d, self.nhi)
        return at, self.device(self.z, at * self.nlo + self.lo, self.core, self.x)

    def along_x(self, d):
        at = lax.rem(self.x + d, self.nx)
        return at, self.device(self.z, self.y, self.core, at)

    def tile(self, d):
        return {"tile": lax.rem(self.t + self.tiles + d, self.tiles), "scan": self.s}

    def partner(self):
        return self.device(self.z, self.y, 1 - self.core, self.x)


def greet(devices):
    barrier = pltpu.get_barrier_semaphore()
    for device in devices:
        pl.semaphore_signal(barrier, inc=1, device_id=device, device_id_type=MESH)
    pl.semaphore_wait(barrier, len(devices))


def sums_kernel(sizes, grad, prb, upd_out, prb_out,
                near, quarter, near2, slim, shifted,
                give, got, mixed, first, held, second, small, third,
                send, recv):
    at = Place(sizes)
    used = [0]
    started = []

    def copy(src, dst, device):
        k = used[0]
        used[0] += 1
        c = pltpu.make_async_remote_copy(
            src_ref=src, dst_ref=dst, send_sem=send.at[k], recv_sem=recv.at[k],
            device_id=device, device_id_type=MESH)
        c.start()
        started.append(c)
        return c

    greet([at.partner(), at.tile(1), at.tile(-1)]
          + [at.along_z(d)[1] for d in range(1, at.nz)]
          + [at.along_y(d)[1] for d in range(1, at.ny)]
          + [at.along_x(d)[1] for d in range(1, at.nx)])

    height, width = grad.shape[1], grad.shape[2]
    xrows = height // at.nx
    hrows = xrows // at.nhi
    total = prb.shape[0]
    half = total // 2
    quart = half // 2

    def block(index, rows):
        return pl.ds(pl.multiple_of(index * rows, 8), rows)

    other_base = (1 - at.core) * half
    my_base = at.core * half

    def cast_half(r):
        give[pl.ds(r, 32), :] = prb[pl.ds(pl.multiple_of(other_base + r, 8), 32), :].astype(BF16)
    rows_loop(half, 32, cast_half)
    p0 = copy(give, got, at.partner())

    o1 = []
    for d in range(1, at.nx):
        to, device = at.along_x(d)
        o1.append(copy(grad.at[:, block(to, xrows), :], near.at[d - 1], device))

    p0.wait_recv()

    def mix(r):
        rows = pl.ds(r, 32)
        mine = prb[pl.ds(pl.multiple_of(my_base + r, 8), 32), :]
        mixed[rows, :] = (mine + got[rows, :].astype(F32)).astype(BF16)
    rows_loop(half, 32, mix)

    axes = ((at.along_z, at.along_y, at.nz, at.ny, at.z, at.y),
            (at.along_y, at.along_z, at.ny, at.nz, at.y, at.z))
    p1 = [[], []]
    for d in range(1, max(at.nz, at.ny)):
        for h, (one, _, n1, n2, c1, c2) in enumerate(axes):
            if d < n1:
                to, device = one(d)
                rows = quart // n1
                src = mixed.at[pl.ds(pl.multiple_of(h * quart + to * rows, 16), rows), :]
                p1[h].append(copy(src, first.at[h, d - 1, pl.ds(0, rows), :], device))

    p2 = [[], []]
    for h, (_, two, n1, n2, c1, c2) in enumerate(axes):
        rows = quart // n1
        for c in p1[h]:
            c.wait_recv()
        base = h * quart + c1 * rows

        def add_first(r, h=h, n1=n1, base=base):
            acc = (prb[pl.ds(pl.multiple_of(my_base + base + r, 8), 16), :]
                   + got[pl.ds(pl.multiple_of(base + r, 16), 16), :].astype(F32))
            for d in range(n1 - 1):
                acc += first[h, d, pl.ds(r, 16), :].astype(F32)
            held[h, pl.ds(r, 16), :] = acc
        rows_loop(rows, 16, add_first)
        sub = rows // n2
        for d in range(1, n2):
            to, device = two(d)
            p2[h].append(copy(held.at[h, block(to, sub), :], second.at[h, d - 1], device))

    for c in o1:
        c.wait_recv()
    xbase = at.x * xrows

    def add_near(r):
        rows = pl.ds(r, 8)
        for k in range(2):
            acc = grad[k, pl.ds(pl.multiple_of(xbase + r, 8), 8), :]
            for d in range(at.nx - 1):
                acc += near[d, k, rows, :]
            quarter[k, rows, :] = acc
    rows_loop(xrows, 8, add_near)
    o2 = []
    for d in range(1, at.nhi):
        to, device = at.along_hi(d)
        o2.append(copy(quarter.at[:, block(to, hrows), :], near2.at[d - 1], device))

    sub = quart // (at.nz * at.ny)
    for h, (_, _, n1, n2, c1, c2) in enumerate(axes):
        for c in p2[h]:
            c.wait_recv()
        acc = held[h, block(c2, sub), :]
        for d in range(n2 - 1):
            acc += second[h, d]
        small[h] = acc
        third[at.x, h] = acc
    p3 = []
    for d in range(1, at.nx):
        _, device = at.along_x(d)
        p3.append(copy(small, third.at[at.x], device))
    for c in p3:
        c.wait_recv()
    p4 = [[], []]
    for h, (_, two, n1, n2, c1, c2) in enumerate(axes):
        acc = third[0, h]
        for k in range(1, at.nx):
            acc += third[k, h]
        rows = pl.ds(pl.multiple_of(my_base + h * quart + c1 * (quart // n1) + c2 * sub, 8), sub)
        prb_out[rows, :] = acc
        for d in range(1, n2):
            p4[h].append(copy(prb_out.at[rows, :], prb_out.at[rows, :], two(d)[1]))

    for c in o2:
        c.wait_recv()
    hbase = at.hi * hrows

    def add_near2(r):
        rows = pl.ds(r, 8)
        for k in (1, 0):
            acc = quarter[k, pl.ds(pl.multiple_of(hbase + r, 8), 8), :]
            for d in range(at.nhi - 1):
                acc += near2[d, k, rows, :]
            slim[k, rows, :] = acc
    rows_loop(hrows, 8, add_near2)
    o0 = copy(slim.at[1], shifted, at.tile(1))

    p5 = [[], []]
    for h, (one, _, n1, n2, c1, c2) in enumerate(axes):
        for c in p4[h]:
            c.wait_recv()
        rows = pl.ds(pl.multiple_of(my_base + h * quart + c1 * (quart // n1), 8), quart // n1)
        for d in range(1, n1):
            p5[h].append(copy(prb_out.at[rows, :], prb_out.at[rows, :], one(d)[1]))

    o0.wait_recv()
    obase = xbase + hbase

    def finish(r):
        upd_out[pl.ds(pl.multiple_of(obase + r, 8), 8), :] = slim[0, pl.ds(r, 8), :] + shifted[pl.ds(r, 8), :]
    rows_loop(hrows, 8, finish)
    o3 = []
    orow = pl.ds(pl.multiple_of(obase, 8), hrows)
    for d in range(1, at.nhi):
        o3.append(copy(upd_out.at[orow, :], upd_out.at[orow, :], at.along_hi(d)[1]))

    p6 = []
    for h, (one, _, n1, n2, c1, c2) in enumerate(axes):
        rows = pl.ds(pl.multiple_of(my_base + h * quart + c1 * (quart // n1), 8), quart // n1)
        p6.append(copy(prb_out.at[rows, :], prb_out.at[rows, :], at.partner()))

    for c in o3:
        c.wait_recv()
    o4 = []
    xrow = pl.ds(pl.multiple_of(xbase, 8), xrows)
    for d in range(1, at.nx):
        o4.append(copy(upd_out.at[xrow, :], upd_out.at[xrow, :], at.along_x(d)[1]))

    for d in range(1, max(at.nz, at.ny)):
        for h, (_, _, n1, n2, c1, c2) in enumerate(axes):
            if d < n1:
                p5[h][d - 1].wait_recv()
                origin = lax.rem(c1 + n1 - d, n1)
                rows = pl.ds(pl.multiple_of(my_base + h * quart + origin * (quart // n1), 8), quart // n1)
                p6.append(copy(prb_out.at[rows, :], prb_out.at[rows, :], at.partner()))
    for c in o4:
        c.wait_recv()
    for c in p6:
        c.wait_recv()
    for c in started:
        c.wait_send()


def count_copies(sizes):
    nz, nlo, nc, nx, nhi = sizes
    ny = nlo * nhi
    return 2 + 2 * (nx - 1) + 2 * (nhi - 1) + 4 * (nz - 1 + ny - 1) + (nx - 1) + (nz + ny)


def sums(sizes, grad, prb):
    nz, nlo, nc, nx, nhi = sizes
    ny = nlo * nhi
    height, width = grad.shape[1:]
    total, pw = prb.shape
    xrows, hrows = height // nx, height // nx // nhi
    half, quart = total // 2, total // 4
    n1, small_n = max(nz, ny), min(nz, ny)
    sub = quart // (nz * ny)
    vmem = pl.BlockSpec(memory_space=pltpu.VMEM)
    copies = count_copies(sizes)
    return pl.pallas_call(
        functools.partial(sums_kernel, sizes),
        out_shape=(jax.ShapeDtypeStruct((height, width), F32), jax.ShapeDtypeStruct((total, pw), F32)),
        in_specs=[vmem, vmem],
        out_specs=(vmem, vmem),
        scratch_shapes=[
            pltpu.VMEM((nx - 1, 2, xrows, width), F32),
            pltpu.VMEM((2, xrows, width), F32),
            pltpu.VMEM((nhi - 1, 2, hrows, width), F32),
            pltpu.VMEM((2, hrows, width), F32),
            pltpu.VMEM((hrows, width), F32),
            pltpu.VMEM((half, pw), BF16),
            pltpu.VMEM((half, pw), BF16),
            pltpu.VMEM((half, pw), BF16),
            pltpu.VMEM((2, n1 - 1, quart // small_n, pw), BF16),
            pltpu.VMEM((2, quart // small_n, pw), F32),
            pltpu.VMEM((2, n1 - 1, sub, pw), F32),
            pltpu.VMEM((2, sub, pw), F32),
            pltpu.VMEM((nx, 2, sub, pw), F32),
            pltpu.SemaphoreType.DMA((copies,)),
            pltpu.SemaphoreType.DMA((copies,)),
        ],
        compiler_params=pltpu.CompilerParams(
            collective_id=1, has_side_effects=True, vmem_limit_bytes=48 << 20),
        name="sums",
    )(grad, prb)


def spread_kernel(sizes, tile, amp, meta, halo, amp_got, meta_got, send, recv):
    at = Place(sizes)
    keep = amp.shape[0] - amp_got.shape[0]
    moved = amp_got.shape[0]
    devices = [at.along_x(d)[1] for d in range(1, moved + 1)]
    greet([at.tile(1), at.tile(-1)] + devices)
    copies = []

    def copy(src, dst, device):
        k = len(copies)
        c = pltpu.make_async_remote_copy(
            src_ref=src, dst_ref=dst, send_sem=send.at[k], recv_sem=recv.at[k],
            device_id=device, device_id_type=MESH)
        c.start()
        copies.append(c)

    copy(tile, halo, at.tile(-1))
    for k, device in enumerate(devices):
        copy(meta, meta_got.at[k], device)
        copy(amp.at[keep + k], amp_got.at[k], device)
    for c in copies:
        c.wait()


def spread(sizes, tile, amp, meta, moved):
    anywhere = pl.BlockSpec(memory_space=pl.ANY)
    return pl.pallas_call(
        functools.partial(spread_kernel, sizes),
        out_shape=(
            jax.ShapeDtypeStruct(tile.shape, tile.dtype),
            jax.ShapeDtypeStruct((moved,) + amp.shape[1:], amp.dtype),
            jax.ShapeDtypeStruct((moved,) + meta.shape, meta.dtype),
        ),
        in_specs=[anywhere] * 3,
        out_specs=(anywhere,) * 3,
        scratch_shapes=[pltpu.SemaphoreType.DMA((1 + 2 * moved,))] * 2,
        compiler_params=pltpu.CompilerParams(collective_id=0, has_side_effects=True),
        name="spread",
    )(tile, amp, meta)


def on_device(object_tiles, probe_modes, amplitudes, row_offsets, col_offsets, slot_counts):
    slots = amplitudes.shape[2]
    edge = (lax.axis_index("tile") == lax.axis_size("tile") - 1).astype(jnp.int32)
    pad = ((0, 0), (0, 128 - slots))
    meta = jnp.concatenate([
        jnp.pad(row_offsets[0], pad),
        jnp.pad(col_offsets[0], pad),
        jnp.full((1, 128), slot_counts[0, 0]),
        jnp.full((1, 128), edge),
        jnp.zeros((4, 128), jnp.int32),
    ])
    halo, amp_got, meta_got = spread(SIZES, object_tiles, amplitudes[0, 0], meta, slots - KEEP)
    grad, probe_grad = positions(
        meta, meta_got, object_tiles, halo, probe_modes, amplitudes[0, 0], amp_got,
        dft_tables(probe_modes.shape[2]),
    )
    width = object_tiles.shape[2]
    update, summed = sums(SIZES, grad.reshape(2, -1, width), probe_grad.reshape(-1, probe_modes.shape[3]))
    new_object = object_tiles + object_step * update.reshape(object_tiles.shape)
    factor = probe_scale / math.sqrt(lax.axis_size("tile") * lax.axis_size("scan"))
    new_probe = probe_modes.astype(F32) + factor * summed.reshape(probe_modes.shape)
    return (new_object, new_probe)


def solution(mesh):
    nz, nlo, nc, nx, nhi = SIZES
    if mesh.shape["tile"] != nz * nlo * nc or mesh.shape["scan"] != nx * nhi:
        raise ValueError("other mesh")
    placed = (
        P(None, None, "tile"),
        P(),
        P("tile", "scan", None, None, None),
        P("tile", "scan", None),
        P("tile", "scan", None),
        P("tile", "scan"),
    )
    return jax.shard_map(
        on_device,
        mesh=mesh,
        in_specs=placed,
        out_specs=(P(None, None, "tile"), P()),
        check_vma=False,
    )
```

```python
import functools
import math

import jax
import jax.numpy as jnp
import numpy as np
from jax import lax
from jax.experimental import pallas as pl
from jax.experimental.pallas import tpu as pltpu
from jax.sharding import PartitionSpec as P

F32, BF16 = jnp.float32, jnp.bfloat16
MESH = pl.DeviceIdType.MESH
KEEP = 2
COPIES = 96
SIZES = (8, 2, 2, 4, 4)
object_step = 0.1
probe_scale = 0.5


def dft_tables(extent):
    index = np.arange(extent)
    angle = (index[:, None] * index[None, :] % extent) * (2.0 * math.pi / extent)
    factor = 1.0 / math.sqrt(extent)
    table = np.stack([np.cos(angle) * factor, -np.sin(angle) * factor])
    return jnp.asarray(table.astype(np.float32)).astype(BF16)


def rows_loop(total, step, body):
    def trip(i, carry):
        body(pl.multiple_of(i * step, step))
        return carry
    lax.fori_loop(0, total // step, trip, 0)


def dot(a, b):
    return jnp.dot(a, b, preferred_element_type=F32)


def positions_kernel(rows_own_in, cols_own_in, count_own_in, rows_got_in, cols_got_in, count_got_in,
                     tile_in, halo, probe_in, amp_own, amp_got, table_in,
                     grad_out, prb_out,
                     rows_own, cols_own, count_own, rows_got, cols_got, count_got, tile, probe, table,
                     amp, lanes, patch, stack, side, wide, term, forward, inverse, arrived, loaded):
    n = probe.shape[2]
    modes = probe.shape[1]
    loads = [
        pltpu.make_async_copy(src, dst, loaded.at[k])
        for k, (src, dst) in enumerate([
            (tile_in, tile), (probe_in, probe), (table_in, table),
            (rows_own_in, rows_own), (cols_own_in, cols_own), (count_own_in, count_own),
            (rows_got_in, rows_got), (cols_got_in, cols_got), (count_got_in, count_got),
        ])
    ]
    for load in loads:
        load.start()
    height, tw = tile.shape[1], tile.shape[2]
    tall = n + 8
    edge = lax.axis_index("tile") == lax.axis_size("tile") - 1

    def clear(at):
        grad_out[:, :, pl.ds(at, 8), :] = jnp.zeros((2, 2, 8, tw), F32)
    rows_loop(height, 8, clear)

    def clear_probe(at):
        prb_out[:, :, pl.ds(at, 8), :] = jnp.zeros((2, modes, 8, n), F32)
    rows_loop(n, 8, clear_probe)

    for load in loads:
        load.wait()
    forward[:n, :n] = table[0]
    forward[n:, n:] = table[0]
    forward[n:, :n] = table[1]
    forward[:n, n:] = -table[1]
    inverse[:n, :n] = table[0]
    inverse[n:, n:] = table[0]
    inverse[n:, :n] = -table[1]
    inverse[:n, n:] = table[1]

    def position(r, c):
        base = pl.multiple_of(jnp.minimum(r // 8 * 8, height - tall), 8)
        rem = r - base
        back_r = tall - rem
        back_c = lax.rem(2 * tw - c, 2 * tw)

        def lane_in(at):
            rows = pl.ds(pl.multiple_of(base + at, 8), 24)
            for p in range(2):
                beside = jnp.where(edge, 0.0, halo[p, rows, :])
                x = jnp.concatenate([tile[p, rows, :], beside], 1)
                lanes[p, pl.ds(at, 24), :] = pltpu.roll(x, back_c, 1)[:, :n]
        rows_loop(tall, 24, lane_in)
        for p in range(2):
            for h in range(n // 128):
                cols = pl.ds(h * 128, 128)
                patch[p, :, cols] = pltpu.roll(lanes[p, :, cols], back_r, 0)[:n]

        def make_psi(at):
            rows, low = pl.ds(at, 16), pl.ds(pl.multiple_of(at + n, 16), 16)
            xr, xi = patch[0, rows, :], patch[1, rows, :]
            for m in range(modes):
                pr = probe[0, m, rows, :].astype(F32)
                pi = probe[1, m, rows, :].astype(F32)
                stack[m, rows, :] = (pr * xr - pi * xi).astype(BF16)
                stack[m, low, :] = (pr * xi + pi * xr).astype(BF16)
        rows_loop(n, 16, make_psi)

        for m in range(modes):
            a = dot(forward[...], stack[m]).astype(BF16)
            side[m, :, :n] = a[:n]
            side[m, :, n:] = a[n:]
        for m in range(modes):
            wide[m] = dot(side[m], inverse[...])

        pltpu.make_async_copy(amp_own.at[0], amp, arrived).wait()

        def make_d(at):
            rows, low = pl.ds(at, 16), pl.ds(pl.multiple_of(at + n, 16), 16)
            total = jnp.zeros((16, n), F32)
            for m in range(modes):
                fr, fi = wide[m, rows, :n], wide[m, rows, n:]
                total += fr * fr + fi * fi
            factor = amp[rows, :].astype(F32) / jnp.sqrt(total + 1.0) - 1.0
            for m in range(modes):
                stack[m, rows, :] = (wide[m, rows, :n] * factor).astype(BF16)
                stack[m, low, :] = (wide[m, rows, n:] * factor).astype(BF16)
        rows_loop(n, 16, make_d)

        for m in range(modes):
            b = dot(inverse[...], stack[m]).astype(BF16)
            side[m, :, :n] = b[:n]
            side[m, :, n:] = b[n:]
        for m in range(modes):
            wide[m] = dot(side[m], forward[...])

        def finish(at):
            rows = pl.ds(at, 16)
            xr, xi = patch[0, rows, :], patch[1, rows, :]
            tr = jnp.zeros((16, n), F32)
            ti = jnp.zeros((16, n), F32)
            for m in range(modes):
                er, ei = wide[m, rows, :n], wide[m, rows, n:]
                pr = probe[0, m, rows, :].astype(F32)
                pi = probe[1, m, rows, :].astype(F32)
                tr += pr * er + pi * ei
                ti += pr * ei - pi * er
                prb_out[0, m, rows, :] += xr * er + xi * ei
                prb_out[1, m, rows, :] += xr * ei - xi * er
            term[0, rows, :] = tr
            term[1, rows, :] = ti
        rows_loop(n, 16, finish)

        term[:, n:, :] = jnp.zeros((2, 8, n), F32)
        for p in range(2):
            for h in range(n // 128):
                cols = pl.ds(h * 128, 128)
                lanes[p, :, cols] = pltpu.roll(term[p, :, cols], rem, 0)

        def lane_out(at):
            rows = pl.ds(pl.multiple_of(base + at, 8), 24)
            for p in range(2):
                y = lanes[p, pl.ds(at, 24), :]
                y = pltpu.roll(jnp.concatenate([y, jnp.zeros_like(y)], 1), c, 1)
                grad_out[0, p, rows, :] += y[:, :tw]
                grad_out[1, p, rows, :] += y[:, tw:]
        rows_loop(tall, 24, lane_out)

    slots = KEEP + amp_got.shape[0]

    def item_trip(item, carry):
        own = item < KEEP
        other = jnp.maximum(item - KEEP, 0)
        r = jnp.where(own, rows_own[0, item], rows_got[other, 0, item])
        c = jnp.where(own, cols_own[0, item], cols_got[other, 0, item])
        count = jnp.where(own, count_own[0, 0], count_got[other, 0, 0])

        @pl.when(item < count)
        def _():
            @pl.when(own)
            def _():
                pltpu.make_async_copy(amp_own.at[item], amp, arrived).start()

            @pl.when(jnp.logical_not(own))
            def _():
                pltpu.make_async_copy(amp_got.at[other], amp, arrived).start()
            position(r, c)
        return carry
    lax.fori_loop(0, slots, item_trip, 0)

    @pl.when(edge)
    def _():
        def drop(at):
            grad_out[1, :, pl.ds(at, 8), :] = jnp.zeros((2, 8, tw), F32)
        rows_loop(height, 8, drop)


def positions(own, got, tile, halo, probe, amp_own, amp_got, table):
    _, modes, n, _ = probe.shape
    height, tw = tile.shape[1:]
    vmem, anywhere = pl.BlockSpec(memory_space=pltpu.VMEM), pl.BlockSpec(memory_space=pl.ANY)
    hbm = pl.BlockSpec(memory_space=pltpu.HBM)
    return pl.pallas_call(
        positions_kernel,
        out_shape=(
            jax.ShapeDtypeStruct((2, 2, height, tw), F32),
            jax.ShapeDtypeStruct((2, modes, n, n), F32),
        ),
        in_specs=[hbm] * 3 + [anywhere] * 3 + [hbm, vmem, hbm, hbm, anywhere, hbm],
        out_specs=(vmem, vmem),
        scratch_shapes=[pltpu.SMEM(m.shape, m.dtype) for m in (*own, *got)] + [
            pltpu.VMEM(tile.shape, F32),
            pltpu.VMEM(probe.shape, BF16),
            pltpu.VMEM(table.shape, BF16),
            pltpu.VMEM((n, n), BF16),
            pltpu.VMEM((2, n + 8, n), F32),
            pltpu.VMEM((2, n, n), F32),
            pltpu.VMEM((modes, 2 * n, n), BF16),
            pltpu.VMEM((modes, n, 2 * n), BF16),
            pltpu.VMEM((modes, n, 2 * n), F32),
            pltpu.VMEM((2, n + 8, n), F32),
            pltpu.VMEM((2 * n, 2 * n), BF16),
            pltpu.VMEM((2 * n, 2 * n), BF16),
            pltpu.SemaphoreType.DMA,
            pltpu.SemaphoreType.DMA((9,)),
        ],
        compiler_params=pltpu.CompilerParams(vmem_limit_bytes=60 * 1024 * 1024),
        name="positions",
    )(*own, *got, tile, halo, probe, amp_own, amp_got, table)


class Place:
    def __init__(self, sizes):
        self.nz, self.nlo, self.nc, self.nx, self.nhi = sizes
        self.ny = self.nlo * self.nhi
        self.tiles, self.scans = self.nz * self.nlo * self.nc, self.nx * self.nhi
        self.t, self.s = lax.axis_index("tile"), lax.axis_index("scan")
        self.core = lax.rem(self.t, self.nc)
        self.lo = lax.rem(self.t // self.nc, self.nlo)
        self.z = self.t // (self.nc * self.nlo)
        self.x, self.hi = self.s // self.nhi, lax.rem(self.s, self.nhi)
        self.y = self.hi * self.nlo + self.lo

    def device(self, z, y, core, x):
        lo, hi = lax.rem(y, self.nlo), y // self.nlo
        return {"tile": (z * self.nlo + lo) * self.nc + core, "scan": x * self.nhi + hi}

    def along_z(self, d):
        at = lax.rem(self.z + d, self.nz)
        return at, self.device(at, self.y, self.core, self.x)

    def along_y(self, d):
        at = lax.rem(self.y + d, self.ny)
        return at, self.device(self.z, at, self.core, self.x)

    def along_hi(self, d):
        at = lax.rem(self.hi + d, self.nhi)
        return at, self.device(self.z, at * self.nlo + self.lo, self.core, self.x)

    def along_x(self, d):
        at = lax.rem(self.x + d, self.nx)
        return at, self.device(self.z, self.y, self.core, at)

    def tile(self, d):
        return {"tile": lax.rem(self.t + self.tiles + d, self.tiles), "scan": self.s}

    def partner(self):
        return self.device(self.z, self.y, 1 - self.core, self.x)


def greet(devices):
    barrier = pltpu.get_barrier_semaphore()
    for device in devices:
        pl.semaphore_signal(barrier, inc=1, device_id=device, device_id_type=MESH)
    pl.semaphore_wait(barrier, len(devices))


def cube(index):
    high, odd = index // 2, lax.rem(index, 2)
    return ((lax.rem(high + odd, 2), index + 1 - 2 * odd), (high, 3 - index))


def sums_kernel(sizes, object_scale, probe_scaling, grad, prb, upd_out, prb_out,
                near1, kept1, near2, kept2, near3, kept3, near4, kept4, shifted,
                give, got, mixed, first, held, second, small, third,
                send, recv):
    at = Place(sizes)
    used = [0]
    started = []

    def copy(src, dst, device):
        k = used[0]
        used[0] += 1
        c = pltpu.make_async_remote_copy(
            src_ref=src, dst_ref=dst, send_sem=send.at[k], recv_sem=recv.at[k],
            device_id=device, device_id_type=MESH)
        c.start()
        started.append(c)
        return c

    greet([at.partner(), at.tile(1), at.tile(-1)]
          + [at.along_z(d)[1] for d in range(1, at.nz)]
          + [at.along_y(d)[1] for d in range(1, at.ny)]
          + [at.along_x(d)[1] for d in range(1, at.nx)])

    height = grad.shape[1]
    total = prb.shape[0]
    half = total // 2
    quart = half // 2

    bits = []
    for h in range(2):
        xb = [(b, at.device(at.z, at.y, at.core, to)) for b, to in cube(at.x)]
        yb = [(b, at.device(at.z, to * at.nlo + at.lo, at.core, at.x)) for b, to in cube(at.hi)]
        bits.append((xb if h == 0 else xb[::-1]) + (yb if h == 0 else yb[::-1]))
    cut = [height // 4, height // 8, height // 16, height // 32]
    near = [near1, near2, near3, near4]
    kept = [kept1, kept2, kept3, kept4]

    def object_source(h, stage):
        if stage == 0:
            return grad, h * (height // 2)
        return kept[stage - 1].at[h], 0

    def object_send(stage):
        out = []
        for h in range(2):
            bit, device = bits[h][stage]
            src, base = object_source(h, stage)
            rows = pl.ds(pl.multiple_of(base + (1 - bit) * cut[stage], 8), cut[stage])
            out.append(copy(src.at[:, rows, :], near[stage].at[h], device))
        return out

    def object_add(stage, copies):
        for h in range(2):
            copies[h].wait_recv()
            bit, _ = bits[h][stage]
            src, base = object_source(h, stage)
            mine = base + bit * cut[stage]

            def add(r, h=h, src=src, mine=mine):
                rows = pl.ds(r, 24)
                for k in range(2):
                    kept[stage][h, k, rows, :] = (
                        src[k, pl.ds(pl.multiple_of(mine + r, 8), 24), :] + near[stage][h, k, rows, :])
            rows_loop(cut[stage], 24, add)

    def object_place(h, stages):
        base = h * (height // 2)
        for stage in range(stages):
            base += bits[h][stage][0] * cut[stage]
        return base

    def object_gather(stage):
        out = []
        for h in range(2):
            rows = pl.ds(pl.multiple_of(object_place(h, stage + 1), 8), cut[stage])
            out.append(copy(upd_out.at[rows, :], upd_out.at[rows, :], bits[h][stage][1]))
        return out

    o = object_send(0)

    other_base = (1 - at.core) * half
    my_base = at.core * half

    def cast_half(r):
        give[pl.ds(r, 32), :] = prb[pl.ds(pl.multiple_of(other_base + r, 8), 32), :].astype(BF16)
    rows_loop(half, 32, cast_half)
    p0 = copy(give, got, at.partner())
    p0.wait_recv()

    def mix(r):
        rows = pl.ds(r, 32)
        mine = prb[pl.ds(pl.multiple_of(my_base + r, 8), 32), :]
        mixed[rows, :] = (mine + got[rows, :].astype(F32)).astype(BF16)
    rows_loop(half, 32, mix)

    axes = ((at.along_z, at.along_y, at.nz, at.ny, at.z, at.y),
            (at.along_y, at.along_z, at.ny, at.nz, at.y, at.z))

    def far_first(n):
        return sorted(range(1, n), key=lambda d: (-min(d, n - d), d))

    p1 = [[], []]
    for h, (one, _, n1, n2, c1, c2) in enumerate(axes):
        for d in far_first(n1):
            to, device = one(d)
            rows = quart // n1
            src = mixed.at[pl.ds(pl.multiple_of(h * quart + to * rows, 16), rows), :]
            p1[h].append(copy(src, first.at[h, d - 1, pl.ds(0, rows), :], device))

    object_add(0, o)
    o = object_send(1)

    p2 = [[], []]
    for h, (_, two, n1, n2, c1, c2) in enumerate(axes):
        rows = quart // n1
        for c in p1[h]:
            c.wait_recv()
        base = h * quart + c1 * rows

        def add_first(r, h=h, n1=n1, base=base):
            acc = (prb[pl.ds(pl.multiple_of(my_base + base + r, 8), 16), :]
                   + got[pl.ds(pl.multiple_of(base + r, 16), 16), :].astype(F32))
            for d in range(n1 - 1):
                acc += first[h, d, pl.ds(r, 16), :].astype(F32)
            held[h, pl.ds(r, 16), :] = acc
        rows_loop(rows, 16, add_first)
        sub = rows // n2
        for d in far_first(n2):
            to, device = two(d)
            src = held.at[h, pl.ds(pl.multiple_of(to * sub, 8), sub), :]
            p2[h].append(copy(src, second.at[h, d - 1], device))

    object_add(1, o)
    o = object_send(2)

    sub = quart // (at.nz * at.ny)
    for h, (_, _, n1, n2, c1, c2) in enumerate(axes):
        for c in p2[h]:
            c.wait_recv()
        acc = held[h, pl.ds(pl.multiple_of(c2 * sub, 8), sub), :]
        for d in range(n2 - 1):
            acc += second[h, d]
        small[h] = acc
        third[at.x, h] = acc
    p3 = [copy(small, third.at[at.x], at.along_x(d)[1]) for d in far_first(at.nx)]
    for c in p3:
        c.wait_recv()
    p4 = [[], []]
    for h, (_, two, n1, n2, c1, c2) in enumerate(axes):
        acc = third[0, h]
        for k in range(1, at.nx):
            acc += third[k, h]
        rows = pl.ds(pl.multiple_of(my_base + h * quart + c1 * (quart // n1) + c2 * sub, 8), sub)
        prb_out[rows, :] = probe_scaling * acc
        for d in far_first(n2):
            p4[h].append(copy(prb_out.at[rows, :], prb_out.at[rows, :], two(d)[1]))

    object_add(2, o)
    o = object_send(3)

    def share(h, origin, device, part=None):
        n1 = axes[h][2]
        size = quart // n1
        base = my_base + h * quart + lax.rem(origin + n1, n1) * size
        if part is not None:
            size = size // 2
            base += part * size
        rows = pl.ds(pl.multiple_of(base, 8), size)
        return copy(prb_out.at[rows, :], prb_out.at[rows, :], device)

    p6 = []
    steps = max(at.nz, at.ny) // 2

    def ring_send(k):
        out = {}
        for h, (one, _, n1, _, c1, _) in enumerate(axes):
            if 2 * k > n1:
                continue
            for side in range(2):
                ahead = one(1 if side == 0 else n1 - 1)[1]
                origin = c1 - (k - 1) if side == 0 else c1 + (k - 1)
                out[h, side] = share(h, origin, ahead, side if 2 * k == n1 else None)
        return out

    def ring_wait(k, sent):
        for h, (one, _, n1, _, c1, _) in enumerate(axes):
            if 2 * k > n1:
                continue
            for side in range(2):
                sent[h, side].wait_recv()

    def ring_share(k):
        for h, (_, _, n1, _, c1, _) in enumerate(axes):
            if 2 * k > n1:
                continue
            p6.append(share(h, c1 - k, at.partner()))
            if 2 * k < n1:
                p6.append(share(h, c1 + k, at.partner()))

    for h in range(2):
        for c in p4[h]:
            c.wait_recv()
    ring = ring_send(1)
    for h in range(2):
        p6.append(share(h, axes[h][4], at.partner()))

    object_add(3, o)
    o = copy(kept4.at[:, 1], shifted, at.tile(1))

    def ring_step(k, ring):
        if k > steps:
            return None
        ring_wait(k, ring)
        after = ring_send(k + 1) if k < steps else None
        ring_share(k)
        return after

    ring = ring_step(1, ring)
    o.wait_recv()
    for h in range(2):
        place = object_place(h, 4)

        def finish(r, h=h, place=place):
            rows = pl.ds(r, 8)
            upd_out[pl.ds(pl.multiple_of(place + r, 8), 8), :] = object_scale * (kept4[h, 0, rows, :] + shifted[h, rows, :])
        rows_loop(cut[3], 8, finish)
    o = object_gather(3)
    ring = ring_step(2, ring)
    for c in o:
        c.wait_recv()
    o = object_gather(2)
    ring = ring_step(3, ring)
    for c in o:
        c.wait_recv()
    o = object_gather(1)
    ring = ring_step(4, ring)
    for c in o:
        c.wait_recv()
    o = object_gather(0)
    for c in o:
        c.wait_recv()
    for c in p6:
        c.wait_recv()
    for c in started:
        c.wait_send()


def sums(sizes, grad, prb, object_scale=1.0, probe_scaling=1.0):
    nz, nlo, nc, nx, nhi = sizes
    ny = nlo * nhi
    height, width = grad.shape[1:]
    total, pw = prb.shape
    half, quart = total // 2, total // 4
    long, short = max(nz, ny), min(nz, ny)
    sub = quart // (nz * ny)
    vmem = pl.BlockSpec(memory_space=pltpu.VMEM)
    stages = []
    for k in (4, 8, 16, 32):
        stages += [pltpu.VMEM((2, 2, height // k, width), F32)] * 2
    return pl.pallas_call(
        functools.partial(sums_kernel, sizes, object_scale, probe_scaling),
        out_shape=(jax.ShapeDtypeStruct((height, width), F32), jax.ShapeDtypeStruct((total, pw), F32)),
        in_specs=[vmem, vmem],
        out_specs=(vmem, vmem),
        scratch_shapes=stages + [
            pltpu.VMEM((2, height // 32, width), F32),
            pltpu.VMEM((half, pw), BF16),
            pltpu.VMEM((half, pw), BF16),
            pltpu.VMEM((half, pw), BF16),
            pltpu.VMEM((2, long - 1, quart // short, pw), BF16),
            pltpu.VMEM((2, quart // short, pw), F32),
            pltpu.VMEM((2, long - 1, sub, pw), F32),
            pltpu.VMEM((2, sub, pw), F32),
            pltpu.VMEM((nx, 2, sub, pw), F32),
            pltpu.SemaphoreType.DMA((COPIES,)),
            pltpu.SemaphoreType.DMA((COPIES,)),
        ],
        compiler_params=pltpu.CompilerParams(
            collective_id=1, has_side_effects=True, vmem_limit_bytes=60 * 1024 * 1024),
        name="sums",
    )(grad, prb)


def spread_kernel(sizes, tile, amp, rows, cols, count, halo, amp_got, rows_got, cols_got, count_got, send, recv):
    at = Place(sizes)
    moved = amp_got.shape[0]
    keep = amp.shape[0] - moved
    devices = [at.along_x(d)[1] for d in range(1, moved + 1)]
    greet([at.tile(1), at.tile(-1)] + devices)
    copies = []

    def copy(src, dst, device):
        k = len(copies)
        c = pltpu.make_async_remote_copy(
            src_ref=src, dst_ref=dst, send_sem=send.at[k], recv_sem=recv.at[k],
            device_id=device, device_id_type=MESH)
        c.start()
        copies.append(c)

    copy(tile, halo, at.tile(-1))
    for k, device in enumerate(devices):
        copy(amp.at[keep + k], amp_got.at[k], device)
        copy(rows, rows_got.at[k], device)
        copy(cols, cols_got.at[k], device)
        copy(count, count_got.at[k], device)
    for c in copies:
        c.wait()


def spread(sizes, moved, tile, amp, *meta):
    anywhere = pl.BlockSpec(memory_space=pl.ANY)
    copies = 1 + (1 + len(meta)) * moved
    return pl.pallas_call(
        functools.partial(spread_kernel, sizes),
        out_shape=(
            jax.ShapeDtypeStruct(tile.shape, tile.dtype),
            jax.ShapeDtypeStruct((moved,) + amp.shape[1:], amp.dtype),
        ) + tuple(jax.ShapeDtypeStruct((moved,) + m.shape, m.dtype) for m in meta),
        in_specs=[pl.BlockSpec(memory_space=pltpu.HBM)] * (2 + len(meta)),
        out_specs=(anywhere,) * (2 + len(meta)),
        scratch_shapes=[pltpu.SemaphoreType.DMA((copies,))] * 2,
        compiler_params=pltpu.CompilerParams(
            collective_id=0, has_side_effects=True, vmem_limit_bytes=60 * 1024 * 1024),
        name="spread",
    )(tile, amp, *meta)


def on_device(object_tiles, probe_modes, amplitudes, row_offsets, col_offsets, slot_counts):
    slots = amplitudes.shape[2]
    meta = (row_offsets[0], col_offsets[0], slot_counts)
    halo, amp_got, *meta_got = spread(SIZES, slots - KEEP, object_tiles, amplitudes[0, 0], *meta)
    grad, probe_grad = positions(
        meta, meta_got, object_tiles, halo, probe_modes, amplitudes[0, 0], amp_got,
        dft_tables(probe_modes.shape[2]),
    )
    width = object_tiles.shape[2]
    factor = probe_scale / math.sqrt(lax.axis_size("tile") * lax.axis_size("scan"))
    update, change = sums(
        SIZES, grad.reshape(2, -1, width), probe_grad.reshape(-1, probe_modes.shape[3]), object_step, factor)
    new_object = object_tiles + update.reshape(object_tiles.shape)
    new_probe = probe_modes.astype(F32) + change.reshape(probe_modes.shape)
    return (new_object, new_probe)


def solution(mesh):
    nz, nlo, nc, nx, nhi = SIZES
    if mesh.shape["tile"] != nz * nlo * nc or mesh.shape["scan"] != nx * nhi:
        raise ValueError("other mesh")
    placed = (
        P(None, None, "tile"),
        P(),
        P("tile", "scan", None, None, None),
        P("tile", "scan", None),
        P("tile", "scan", None),
        P("tile", "scan"),
    )
    return jax.shard_map(
        on_device,
        mesh=mesh,
        in_specs=placed,
        out_specs=(P(None, None, "tile"), P()),
        check_vma=False,
    )
```

```python
import functools
import math

import jax
import jax.numpy as jnp
import numpy as np
from jax import lax
from jax.experimental import pallas as pl
from jax.experimental.pallas import tpu as pltpu
from jax.sharding import PartitionSpec as P

F32, BF16 = jnp.float32, jnp.bfloat16
MESH = pl.DeviceIdType.MESH
KEEP = 2
COPIES = 136
ORDER = "rlpprlprlprlrlplrplpplpplpplpplpllpppppppllllllllll"
SIZES = (8, 2, 2, 4, 4)
object_step = 0.1
probe_scale = 0.5


def dft_tables(extent):
    index = np.arange(extent)
    angle = (index[:, None] * index[None, :] % extent) * (2.0 * math.pi / extent)
    factor = 1.0 / math.sqrt(extent)
    table = np.stack([np.cos(angle) * factor, -np.sin(angle) * factor])
    return jnp.asarray(table.astype(np.float32)).astype(BF16)


def rows_loop(total, step, body, unroll=1):
    def trip(i, carry):
        body(pl.multiple_of(i * step, step))
        return carry
    lax.fori_loop(0, total // step, trip, 0, unroll=unroll)


def dot(a, b):
    return jnp.dot(a, b, preferred_element_type=F32)


def positions_kernel(rows_own_in, cols_own_in, count_own_in, rows_got_in, cols_got_in, count_got_in,
                     tile_in, halo_in, probe_in, amp_own, amp_got, table_in,
                     grad_out, prb_out,
                     rows_own, cols_own, count_own, rows_got, cols_got, count_got, ext, probe, table,
                     amp, patch, stack, side, wide, term, forward, inverse, arrived, loaded):
    n = probe.shape[2]
    modes = probe.shape[1]
    blocks, _, height, lane = grad_out.shape
    near, inner = blocks // 2, n // lane
    moves = [(tile_in.at[:, :, pl.ds(b * lane, lane)], ext.at[b]) for b in range(near)]
    moves += [(halo_in.at[:, :, pl.ds(b * lane, lane)], ext.at[near + b]) for b in range(near)]
    moves += [
        (probe_in, probe), (table_in, table),
        (rows_own_in, rows_own), (cols_own_in, cols_own), (count_own_in, count_own),
        (rows_got_in, rows_got), (cols_got_in, cols_got), (count_got_in, count_got),
    ]
    loads = [pltpu.make_async_copy(src, dst, loaded.at[k]) for k, (src, dst) in enumerate(moves)]
    for load in loads:
        load.start()
    edge = lax.axis_index("tile") == lax.axis_size("tile") - 1

    def clear(at):
        grad_out[:, :, pl.ds(at, 16), :] = jnp.zeros((blocks, 2, 16, lane), F32)
    rows_loop(height, 16, clear)

    def clear_probe(at):
        prb_out[:, :, pl.ds(at, 16), :] = jnp.zeros((2, modes, 16, n), F32)
    rows_loop(n, 16, clear_probe)
    term[:, :8, :] = jnp.zeros((2, 8, n), F32)
    term[:, n + 8:, :] = jnp.zeros((2, 8, n), F32)
    for load in loads:
        load.wait()

    @pl.when(edge)
    def _():
        def drop(at):
            ext[near:, :, pl.ds(at, 16), :] = jnp.zeros((blocks - near, 2, 16, lane), F32)
        rows_loop(height, 16, drop)
    forward[:n, :n] = table[0]
    forward[n:, n:] = table[0]
    forward[n:, :n] = table[1]
    forward[:n, n:] = -table[1]
    inverse[:n, :n] = table[0]
    inverse[n:, n:] = table[0]
    inverse[n:, :n] = -table[1]
    inverse[:n, n:] = table[1]

    def position(r, c):
        base = pl.multiple_of(jnp.minimum(r // 8 * 8, height - n - 8), 8)
        down = r - base
        block, right = c // lane, lax.rem(c, lane)
        up, left = lax.rem(8 - down, 8), lax.rem(lane - right, lane)
        lanes = lax.broadcasted_iota(jnp.int32, (8, lane), 1)
        rows8 = lax.broadcasted_iota(jnp.int32, (8, lane), 0)
        in_lanes, in_rows = lanes < lane - right, rows8 < 8 - down
        out_lanes, out_rows = lanes >= right, rows8 >= down

        def cut(at):
            for p in range(2):
                turned = [
                    pltpu.roll(ext[block + j, p, pl.ds(pl.multiple_of(base + at, 8), 40), :], left, 1).reshape(5, 8, lane)
                    for j in range(inner + 1)
                ]
                for j in range(inner):
                    x = jnp.where(in_lanes, turned[j], turned[j + 1])
                    x = pltpu.roll(x, up, 1)
                    x = jnp.where(in_rows, x[:4], x[1:])
                    patch[p, pl.ds(at, 32), j * lane:(j + 1) * lane] = x.reshape(32, lane)
        rows_loop(n, 32, cut, unroll=True)

        def make_psi(at):
            rows, low = pl.ds(at, 16), pl.ds(pl.multiple_of(at + n, 16), 16)
            xr, xi = patch[0, rows, :], patch[1, rows, :]
            for m in range(modes):
                pr = probe[0, m, rows, :].astype(F32)
                pi = probe[1, m, rows, :].astype(F32)
                stack[m, rows, :] = (pr * xr - pi * xi).astype(BF16)
                stack[m, low, :] = (pr * xi + pi * xr).astype(BF16)
        rows_loop(n, 16, make_psi, unroll=True)

        for m in range(modes):
            a = dot(forward[...], stack[m]).astype(BF16)
            side[m, :, :n] = a[:n]
            side[m, :, n:] = a[n:]
        for m in range(modes):
            wide[m] = dot(side[m], inverse[...])

        pltpu.make_async_copy(amp_own.at[0], amp, arrived).wait()

        def make_d(at):
            rows, low = pl.ds(at, 16), pl.ds(pl.multiple_of(at + n, 16), 16)
            total = jnp.zeros((16, n), F32)
            for m in range(modes):
                fr, fi = wide[m, rows, :n], wide[m, rows, n:]
                total += fr * fr + fi * fi
            factor = amp[rows, :].astype(F32) / jnp.sqrt(total + 1.0) - 1.0
            for m in range(modes):
                stack[m, rows, :] = (wide[m, rows, :n] * factor).astype(BF16)
                stack[m, low, :] = (wide[m, rows, n:] * factor).astype(BF16)
        rows_loop(n, 16, make_d, unroll=True)

        for m in range(modes):
            b = dot(inverse[...], stack[m]).astype(BF16)
            side[m, :, :n] = b[:n]
            side[m, :, n:] = b[n:]
        for m in range(modes):
            wide[m] = dot(side[m], forward[...])

        def finish(at):
            rows = pl.ds(at, 16)
            xr, xi = patch[0, rows, :], patch[1, rows, :]
            tr = jnp.zeros((16, n), F32)
            ti = jnp.zeros((16, n), F32)
            for m in range(modes):
                er, ei = wide[m, rows, :n], wide[m, rows, n:]
                pr = probe[0, m, rows, :].astype(F32)
                pi = probe[1, m, rows, :].astype(F32)
                tr += pr * er + pi * ei
                ti += pr * ei - pi * er
                prb_out[0, m, rows, :] += xr * er + xi * ei
                prb_out[1, m, rows, :] += xr * ei - xi * er
            below = pl.ds(pl.multiple_of(at + 8, 8), 16)
            term[0, below, :] = tr
            term[1, below, :] = ti
        rows_loop(n, 16, finish, unroll=True)

        def paste(at):
            rows = pl.ds(pl.multiple_of(base + at, 8), 24)
            for p in range(2):
                turned = []
                for j in range(inner):
                    x = term[p, pl.ds(at, 32), j * lane:(j + 1) * lane].reshape(4, 8, lane)
                    x = pltpu.roll(x, lax.rem(down, 8), 1)
                    x = jnp.where(out_rows, x[1:], x[:3]).reshape(24, lane)
                    turned.append(pltpu.roll(x, right, 1).reshape(3, 8, lane))
                for j in range(inner + 1):
                    low = turned[j] if j < inner else jnp.zeros((3, 8, lane), F32)
                    high = turned[j - 1] if j > 0 else jnp.zeros((3, 8, lane), F32)
                    grad_out[block + j, p, rows, :] += jnp.where(out_lanes, low, high).reshape(24, lane)
        rows_loop(n + 8, 24, paste, unroll=True)

    slots = KEEP + amp_got.shape[0]

    def item_trip(item, carry):
        own = item < KEEP
        other = jnp.maximum(item - KEEP, 0)
        r = jnp.where(own, rows_own[0, item], rows_got[other, 0, item])
        c = jnp.where(own, cols_own[0, item], cols_got[other, 0, item])
        count = jnp.where(own, count_own[0, 0], count_got[other, 0, 0])

        @pl.when(item < count)
        def _():
            @pl.when(own)
            def _():
                pltpu.make_async_copy(amp_own.at[item], amp, arrived).start()

            @pl.when(jnp.logical_not(own))
            def _():
                pltpu.make_async_copy(amp_got.at[other], amp, arrived).start()
            position(r, c)
        return carry
    lax.fori_loop(0, slots, item_trip, 0)

    @pl.when(edge)
    def _():
        def drop(at):
            grad_out[near:, :, pl.ds(at, 16), :] = jnp.zeros((blocks - near, 2, 16, lane), F32)
        rows_loop(height, 16, drop)


def positions(own, got, tile, halo, probe, amp_own, amp_got, table):
    _, modes, n, _ = probe.shape
    height, tw = tile.shape[1:]
    vmem, anywhere = pl.BlockSpec(memory_space=pltpu.VMEM), pl.BlockSpec(memory_space=pl.ANY)
    hbm = pl.BlockSpec(memory_space=pltpu.HBM)
    return pl.pallas_call(
        positions_kernel,
        out_shape=(
            jax.ShapeDtypeStruct((2 * tw // 128, 2, height, 128), F32),
            jax.ShapeDtypeStruct((2, modes, n, n), F32),
        ),
        in_specs=[hbm] * 3 + [anywhere] * 3 + [hbm, anywhere, hbm, hbm, anywhere, hbm],
        out_specs=(vmem, vmem),
        scratch_shapes=[pltpu.SMEM(m.shape, m.dtype) for m in (*own, *got)] + [
            pltpu.VMEM((2 * tw // 128, 2, height, 128), F32),
            pltpu.VMEM(probe.shape, BF16),
            pltpu.VMEM(table.shape, BF16),
            pltpu.VMEM((n, n), BF16),
            pltpu.VMEM((2, n, n), F32),
            pltpu.VMEM((modes, 2 * n, n), BF16),
            pltpu.VMEM((modes, n, 2 * n), BF16),
            pltpu.VMEM((modes, n, 2 * n), F32),
            pltpu.VMEM((2, n + 16, n), F32),
            pltpu.VMEM((2 * n, 2 * n), BF16),
            pltpu.VMEM((2 * n, 2 * n), BF16),
            pltpu.SemaphoreType.DMA,
            pltpu.SemaphoreType.DMA((8 + 2 * tw // 128,)),
        ],
        compiler_params=pltpu.CompilerParams(vmem_limit_bytes=60 * 1024 * 1024),
        name="positions",
    )(*own, *got, tile, halo, probe, amp_own, amp_got, table)


class Place:
    def __init__(self, sizes):
        self.nz, self.nlo, self.nc, self.nx, self.nhi = sizes
        self.ny = self.nlo * self.nhi
        self.tiles, self.scans = self.nz * self.nlo * self.nc, self.nx * self.nhi
        self.t, self.s = lax.axis_index("tile"), lax.axis_index("scan")
        self.core = lax.rem(self.t, self.nc)
        self.lo = lax.rem(self.t // self.nc, self.nlo)
        self.z = self.t // (self.nc * self.nlo)
        self.x, self.hi = self.s // self.nhi, lax.rem(self.s, self.nhi)
        self.y = self.hi * self.nlo + self.lo

    def device(self, z, y, core, x):
        lo, hi = lax.rem(y, self.nlo), y // self.nlo
        return {"tile": (z * self.nlo + lo) * self.nc + core, "scan": x * self.nhi + hi}

    def along_z(self, d):
        at = lax.rem(self.z + d, self.nz)
        return at, self.device(at, self.y, self.core, self.x)

    def along_y(self, d):
        at = lax.rem(self.y + d, self.ny)
        return at, self.device(self.z, at, self.core, self.x)

    def along_hi(self, d):
        at = lax.rem(self.hi + d, self.nhi)
        return at, self.device(self.z, at * self.nlo + self.lo, self.core, self.x)

    def along_x(self, d):
        at = lax.rem(self.x + d, self.nx)
        return at, self.device(self.z, self.y, self.core, at)

    def tile(self, d):
        return {"tile": lax.rem(self.t + self.tiles + d, self.tiles), "scan": self.s}

    def partner(self):
        return self.device(self.z, self.y, 1 - self.core, self.x)


def greet(devices):
    barrier = pltpu.get_barrier_semaphore()
    for device in devices:
        pl.semaphore_signal(barrier, inc=1, device_id=device, device_id_type=MESH)
    pl.semaphore_wait(barrier, len(devices))


def cube(index):
    high, odd = index // 2, lax.rem(index, 2)
    return ((lax.rem(high + odd, 2), index + 1 - 2 * odd), (high, 3 - index))


def sums_kernel(sizes, object_scale, probe_scaling, grad, prb, upd_low, upd_high, prb_out,
                near1, kept1, near2, kept2, near3, kept3, near4, kept4, shifted,
                give, got, mixed, first, held, second, small, third,
                send, recv):
    at = Place(sizes)
    used = [0]
    started = []

    def copy(src, dst, device):
        k = used[0]
        used[0] += 1
        c = pltpu.make_async_remote_copy(
            src_ref=src, dst_ref=dst, send_sem=send.at[k], recv_sem=recv.at[k],
            device_id=device, device_id_type=MESH)
        c.start()
        started.append(c)
        return c

    greet([at.partner(), at.tile(1), at.tile(-1)]
          + [at.along_z(d)[1] for d in range(1, at.nz)]
          + [at.along_y(d)[1] for d in range(1, at.ny)]
          + [at.along_x(d)[1] for d in range(1, at.nx)])

    height = grad.shape[1]
    total = prb.shape[0]
    half = total // 2
    quart = half // 2

    bits = []
    for h in range(2):
        xb = [(b, at.device(at.z, at.y, at.core, to)) for b, to in cube(at.x)]
        yb = [(b, at.device(at.z, to * at.nlo + at.lo, at.core, at.x)) for b, to in cube(at.hi)]
        bits.append((xb if h == 0 else xb[::-1]) + (yb if h == 0 else yb[::-1]))
    cut = [height // 4, height // 8, height // 16, height // 32]
    near = [near1, near2, near3, near4]
    kept = [kept1, kept2, kept3, kept4]

    def object_source(side, h, stage):
        if stage == 0:
            return grad.at[side], h * (height // 2)
        return kept[stage - 1].at[h, side], 0

    def object_send(side, stage):
        out = []
        for h in range(2):
            bit, device = bits[h][stage]
            src, base = object_source(side, h, stage)
            rows = pl.ds(pl.multiple_of(base + (1 - bit) * cut[stage], 8), cut[stage])
            out.append(copy(src.at[rows, :], near[stage].at[h, side], device))
        return out

    def object_add(side, stage, copies):
        for h in range(2):
            copies[h].wait_recv()
            bit, _ = bits[h][stage]
            src, base = object_source(side, h, stage)
            mine = base + bit * cut[stage]

            def add(r, h=h, src=src, mine=mine):
                rows = pl.ds(r, 48)
                kept[stage][h, side, rows, :] = (
                    src[pl.ds(pl.multiple_of(mine + r, 8), 48), :] + near[stage][h, side, rows, :])
            rows_loop(cut[stage], 48, add, unroll=True)

    upd_out = (upd_low, upd_high)

    def object_place(h, stages):
        base = 0
        for stage in range(stages):
            base += bits[h][stage][0] * cut[stage]
        return base

    def object_gather(stage):
        out = []
        for h in range(2):
            rows = pl.ds(pl.multiple_of(object_place(h, stage + 1), 8), cut[stage])
            out.append(copy(upd_out[h].at[rows, :], upd_out[h].at[rows, :], bits[h][stage][1]))
        return out

    crossing = []

    def objects(side):
        o = object_send(side, 0)
        for stage in range(3):
            yield
            object_add(side, stage, o)
            o = object_send(side, stage + 1)
        yield
        object_add(side, 3, o)
        if side == 1:
            crossing.append(copy(kept4.at[:, 1], shifted, at.tile(1)))
            return
        yield
        crossing[0].wait_recv()
        for h in range(2):
            place = object_place(h, 4)

            def finish(r, h=h, place=place):
                rows = pl.ds(r, 48)
                upd_out[h][pl.ds(pl.multiple_of(place + r, 8), 48), :] = object_scale * (
                    kept4[h, 0, rows, :] + shifted[h, rows, :])
            rows_loop(cut[3], 48, finish)
        for stage in (3, 2, 1, 0):
            o = object_gather(stage)
            yield
            for c in o:
                c.wait_recv()

    axes = ((at.along_z, at.along_y, at.nz, at.ny, at.z, at.y),
            (at.along_y, at.along_z, at.ny, at.nz, at.y, at.z))

    def far_first(n):
        return sorted(range(1, n), key=lambda d: (-min(d, n - d), d))

    def share(h, origin, device, part=None):
        n1 = axes[h][2]
        size = quart // n1
        base = my_base + h * quart + lax.rem(origin + n1, n1) * size
        if part is not None:
            size = size // 2
            base += part * size
        rows = pl.ds(pl.multiple_of(base, 8), size)
        return copy(prb_out.at[rows, :], prb_out.at[rows, :], device)

    other_base = (1 - at.core) * half
    my_base = at.core * half
    sub = quart // (at.nz * at.ny)

    def probes():
        def cast_half(r):
            give[pl.ds(r, 32), :] = prb[pl.ds(pl.multiple_of(other_base + r, 8), 32), :].astype(BF16)
        rows_loop(half, 32, cast_half, unroll=4)
        p0 = copy(give, got, at.partner())
        yield
        p0.wait_recv()

        def mix(r):
            rows = pl.ds(r, 32)
            mine = prb[pl.ds(pl.multiple_of(my_base + r, 8), 32), :]
            mixed[rows, :] = (mine + got[rows, :].astype(F32)).astype(BF16)
        rows_loop(half, 32, mix, unroll=4)
        p1 = [[], []]
        for h, (one, _, n1, n2, c1, c2) in enumerate(axes):
            for d in far_first(n1):
                to, device = one(d)
                rows = quart // n1
                src = mixed.at[pl.ds(pl.multiple_of(h * quart + to * rows, 16), rows), :]
                p1[h].append(copy(src, first.at[h, d - 1, pl.ds(0, rows), :], device))
        yield
        p2 = [[], []]
        for h, (_, two, n1, n2, c1, c2) in enumerate(axes):
            rows = quart // n1
            for c in p1[h]:
                c.wait_recv()
            base = h * quart + c1 * rows

            def add_first(r, h=h, n1=n1, base=base):
                acc = (prb[pl.ds(pl.multiple_of(my_base + base + r, 8), 16), :]
                       + got[pl.ds(pl.multiple_of(base + r, 16), 16), :].astype(F32))
                for d in range(n1 - 1):
                    acc += first[h, d, pl.ds(r, 16), :].astype(F32)
                held[h, pl.ds(r, 16), :] = acc
            rows_loop(rows, 16, add_first, unroll=True)
            for d in far_first(n2):
                to, device = two(d)
                src = held.at[h, pl.ds(pl.multiple_of(to * sub, 8), sub), :]
                p2[h].append(copy(src, second.at[h, d - 1], device))
        yield
        for h, (_, _, n1, n2, c1, c2) in enumerate(axes):
            for c in p2[h]:
                c.wait_recv()
            acc = held[h, pl.ds(pl.multiple_of(c2 * sub, 8), sub), :]
            for d in range(n2 - 1):
                acc += second[h, d]
            small[h] = acc
            third[at.x, h] = acc
        p3 = [copy(small, third.at[at.x], at.along_x(d)[1]) for d in far_first(at.nx)]
        yield
        for c in p3:
            c.wait_recv()
        p4 = [[], []]
        for h, (_, two, n1, n2, c1, c2) in enumerate(axes):
            acc = third[0, h]
            for k in range(1, at.nx):
                acc += third[k, h]
            rows = pl.ds(pl.multiple_of(my_base + h * quart + c1 * (quart // n1) + c2 * sub, 8), sub)
            prb_out[rows, :] = probe_scaling * acc
            for d in far_first(n2):
                p4[h].append(copy(prb_out.at[rows, :], prb_out.at[rows, :], two(d)[1]))
        yield
        for h in range(2):
            for c in p4[h]:
                c.wait_recv()
        p6 = []
        steps = max(at.nz, at.ny) // 2

        def ring_send(k, part):
            out = {}
            for h, (one, _, n1, _, c1, _) in enumerate(axes):
                for side in range(2):
                    if 2 * k < n1 or (2 * k == n1 and side == part):
                        ahead = one(1 if side == 0 else n1 - 1)[1]
                        out[h, side] = share(h, c1 - (k - 1) if side == 0 else c1 + (k - 1), ahead, part)
            return out

        ring = [ring_send(1, part) for part in range(2)]
        for h in range(2):
            p6.append(share(h, axes[h][4], at.partner()))
        for k in range(1, steps + 1):
            for part in range(2):
                yield
                for c in ring[part].values():
                    c.wait_recv()
                passed = ring[part]
                ring[part] = ring_send(k + 1, part) if k < steps else {}
                for h, side in passed:
                    p6.append(share(h, axes[h][4] - k if side == 0 else axes[h][4] + k, at.partner(), part))
        yield
        for c in p6:
            c.wait_recv()

    chains = {"r": objects(1), "l": objects(0), "p": probes()}
    for turn in ORDER:
        next(chains[turn], None)
    for c in started:
        c.wait_send()


def sums(sizes, grad, prb, object_scale=1.0, probe_scaling=1.0):
    nz, nlo, nc, nx, nhi = sizes
    ny = nlo * nhi
    height, width = grad.shape[1:]
    total, pw = prb.shape
    half, quart = total // 2, total // 4
    long, short = max(nz, ny), min(nz, ny)
    sub = quart // (nz * ny)
    vmem = pl.BlockSpec(memory_space=pltpu.VMEM)
    stages = []
    for k in (4, 8, 16, 32):
        stages += [pltpu.VMEM((2, 2, height // k, width), F32)] * 2
    return pl.pallas_call(
        functools.partial(sums_kernel, sizes, object_scale, probe_scaling),
        out_shape=(
            jax.ShapeDtypeStruct((height // 2, width), F32),
            jax.ShapeDtypeStruct((height // 2, width), F32),
            jax.ShapeDtypeStruct((total, pw), F32),
        ),
        in_specs=[vmem, vmem],
        out_specs=(vmem, vmem, vmem),
        scratch_shapes=stages + [
            pltpu.VMEM((2, height // 32, width), F32),
            pltpu.VMEM((half, pw), BF16),
            pltpu.VMEM((half, pw), BF16),
            pltpu.VMEM((half, pw), BF16),
            pltpu.VMEM((2, long - 1, quart // short, pw), BF16),
            pltpu.VMEM((2, quart // short, pw), F32),
            pltpu.VMEM((2, long - 1, sub, pw), F32),
            pltpu.VMEM((2, sub, pw), F32),
            pltpu.VMEM((nx, 2, sub, pw), F32),
            pltpu.SemaphoreType.DMA((COPIES,)),
            pltpu.SemaphoreType.DMA((COPIES,)),
        ],
        compiler_params=pltpu.CompilerParams(
            collective_id=1, has_side_effects=True, vmem_limit_bytes=40 << 20),
        name="sums",
    )(grad, prb)


def spread_kernel(sizes, tile, amp, rows, cols, count, halo, amp_got, rows_got, cols_got, count_got, send, recv):
    at = Place(sizes)
    moved = amp_got.shape[0]
    keep = amp.shape[0] - moved
    devices = [at.along_x(d)[1] for d in range(1, moved + 1)]
    greet([at.tile(1), at.tile(-1)] + devices)
    copies = []

    def copy(src, dst, device):
        k = len(copies)
        c = pltpu.make_async_remote_copy(
            src_ref=src, dst_ref=dst, send_sem=send.at[k], recv_sem=recv.at[k],
            device_id=device, device_id_type=MESH)
        c.start()
        copies.append(c)

    copy(tile, halo, at.tile(-1))
    for k, device in enumerate(devices):
        copy(amp.at[keep + k], amp_got.at[k], device)
        copy(rows, rows_got.at[k], device)
        copy(cols, cols_got.at[k], device)
        copy(count, count_got.at[k], device)
    for c in copies:
        c.wait()


def spread(sizes, moved, tile, amp, *meta):
    anywhere = pl.BlockSpec(memory_space=pl.ANY)
    copies = 1 + (1 + len(meta)) * moved
    return pl.pallas_call(
        functools.partial(spread_kernel, sizes),
        out_shape=(
            jax.ShapeDtypeStruct(tile.shape, tile.dtype),
            jax.ShapeDtypeStruct((moved,) + amp.shape[1:], amp.dtype),
        ) + tuple(jax.ShapeDtypeStruct((moved,) + m.shape, m.dtype) for m in meta),
        in_specs=[pl.BlockSpec(memory_space=pltpu.HBM)] * (2 + len(meta)),
        out_specs=(anywhere,) * (2 + len(meta)),
        scratch_shapes=[pltpu.SemaphoreType.DMA((copies,))] * 2,
        compiler_params=pltpu.CompilerParams(
            collective_id=0, has_side_effects=True, vmem_limit_bytes=60 * 1024 * 1024),
        name="spread",
    )(tile, amp, *meta)


def on_device(object_tiles, probe_modes, amplitudes, row_offsets, col_offsets, slot_counts):
    slots = amplitudes.shape[2]
    meta = (row_offsets[0], col_offsets[0], slot_counts)
    halo, amp_got, *meta_got = spread(SIZES, slots - KEEP, object_tiles, amplitudes[0, 0], *meta)
    grad, probe_grad = positions(
        meta, meta_got, object_tiles, halo, probe_modes, amplitudes[0, 0], amp_got,
        dft_tables(probe_modes.shape[2]),
    )
    factor = probe_scale / math.sqrt(lax.axis_size("tile") * lax.axis_size("scan"))
    blocks, _, height, lane = grad.shape
    *update, change = sums(
        SIZES, grad.reshape(2, -1, lane), probe_grad.reshape(-1, probe_modes.shape[3]), object_step, factor)
    update = jnp.concatenate([u.reshape(2, height, lane) for u in update], axis=2)
    new_object = object_tiles + update
    new_probe = probe_modes.astype(F32) + change.reshape(probe_modes.shape)
    return (new_object, new_probe)


def solution(mesh):
    nz, nlo, nc, nx, nhi = SIZES
    if mesh.shape["tile"] != nz * nlo * nc or mesh.shape["scan"] != nx * nhi:
        raise ValueError("other mesh")
    placed = (
        P(None, None, "tile"),
        P(),
        P("tile", "scan", None, None, None),
        P("tile", "scan", None),
        P("tile", "scan", None),
        P("tile", "scan"),
    )
    return jax.shard_map(
        on_device,
        mesh=mesh,
        in_specs=placed,
        out_specs=(P(None, None, "tile"), P()),
        check_vma=False,
    )
```

```python
import functools
import math

import jax
import jax.numpy as jnp
import numpy as np
from jax import lax
from jax.experimental import pallas as pl
from jax.experimental.pallas import tpu as pltpu
from jax.sharding import PartitionSpec as P

F32, BF16 = jnp.float32, jnp.bfloat16
MESH = pl.DeviceIdType.MESH
KEEP = 2
COPIES = 136
ORDER = "rlpprlprlprlrlplrplpplpplpplpplpllpppppppllllllllll"
SIZES = (8, 2, 2, 4, 4)
object_step = 0.1
probe_scale = 0.5


def dft_tables(extent):
    index = np.arange(extent)
    angle = (index[:, None] * index[None, :] % extent) * (2.0 * math.pi / extent)
    factor = 1.0 / math.sqrt(extent)
    table = np.stack([np.cos(angle) * factor, -np.sin(angle) * factor])
    return jnp.asarray(table.astype(np.float32)).astype(BF16)


def rows_loop(total, step, body, unroll=1):
    def trip(i, carry):
        body(pl.multiple_of(i * step, step))
        return carry
    lax.fori_loop(0, total // step, trip, 0, unroll=unroll)


def dot(a, b):
    return jnp.dot(a, b, preferred_element_type=F32)


def positions_kernel(rows_own_in, cols_own_in, count_own_in, rows_got_in, cols_got_in, count_got_in,
                     tile_in, halo_in, probe_in, amp_own, amp_got, table_in,
                     grad_out, prb_out,
                     rows_own, cols_own, count_own, rows_got, cols_got, count_got, ext, probe, table,
                     amp, patch, stack, side, wide, term, forward, inverse, arrived, loaded):
    n = probe.shape[2]
    modes = probe.shape[1]
    blocks, _, height, lane = grad_out.shape
    near, inner = blocks // 2, n // lane
    moves = [(tile_in.at[:, :, pl.ds(b * lane, lane)], ext.at[b]) for b in range(near)]
    moves += [(halo_in.at[:, :, pl.ds(b * lane, lane)], ext.at[near + b]) for b in range(near)]
    moves += [
        (probe_in, probe), (table_in, table),
        (rows_own_in, rows_own), (cols_own_in, cols_own), (count_own_in, count_own),
        (rows_got_in, rows_got), (cols_got_in, cols_got), (count_got_in, count_got),
    ]
    loads = [pltpu.make_async_copy(src, dst, loaded.at[k]) for k, (src, dst) in enumerate(moves)]
    for load in loads:
        load.start()
    edge = lax.axis_index("tile") == lax.axis_size("tile") - 1

    def clear(at):
        grad_out[:, :, pl.ds(at, 16), :] = jnp.zeros((blocks, 2, 16, lane), F32)
    rows_loop(height, 16, clear)

    def clear_probe(at):
        prb_out[:, :, pl.ds(at, 16), :] = jnp.zeros((2, modes, 16, n), F32)
    rows_loop(n, 16, clear_probe)
    term[:, :8, :] = jnp.zeros((2, 8, n), F32)
    term[:, n + 8:, :] = jnp.zeros((2, 8, n), F32)
    for load in loads:
        load.wait()

    @pl.when(edge)
    def _():
        def drop(at):
            ext[near:, :, pl.ds(at, 16), :] = jnp.zeros((blocks - near, 2, 16, lane), F32)
        rows_loop(height, 16, drop)
    forward[:n, :n] = table[0]
    forward[n:, n:] = table[0]
    forward[n:, :n] = table[1]
    forward[:n, n:] = -table[1]
    inverse[:n, :n] = table[0]
    inverse[n:, n:] = table[0]
    inverse[n:, :n] = -table[1]
    inverse[:n, n:] = table[1]

    def position(r, c):
        base = pl.multiple_of(jnp.minimum(r // 8 * 8, height - n - 8), 8)
        down = r - base
        block, right = c // lane, lax.rem(c, lane)
        up, left = lax.rem(8 - down, 8), lax.rem(lane - right, lane)
        lanes = lax.broadcasted_iota(jnp.int32, (8, lane), 1)
        rows8 = lax.broadcasted_iota(jnp.int32, (8, lane), 0)
        in_lanes, in_rows = lanes < lane - right, rows8 < 8 - down
        out_lanes, out_rows = lanes >= right, rows8 >= down

        def cut(at):
            for p in range(2):
                turned = [
                    pltpu.roll(ext[block + j, p, pl.ds(pl.multiple_of(base + at, 8), 40), :], left, 1).reshape(5, 8, lane)
                    for j in range(inner + 1)
                ]
                for j in range(inner):
                    x = jnp.where(in_lanes, turned[j], turned[j + 1])
                    x = pltpu.roll(x, up, 1)
                    x = jnp.where(in_rows, x[:4], x[1:])
                    patch[p, pl.ds(at, 32), j * lane:(j + 1) * lane] = x.reshape(32, lane)
        rows_loop(n, 32, cut, unroll=True)

        def make_psi(at):
            rows, low = pl.ds(at, 16), pl.ds(pl.multiple_of(at + n, 16), 16)
            xr, xi = patch[0, rows, :], patch[1, rows, :]
            for m in range(modes):
                pr = probe[0, m, rows, :].astype(F32)
                pi = probe[1, m, rows, :].astype(F32)
                stack[m, rows, :] = (pr * xr - pi * xi).astype(BF16)
                stack[m, low, :] = (pr * xi + pi * xr).astype(BF16)
        rows_loop(n, 16, make_psi, unroll=True)

        for m in range(modes):
            a = dot(forward[...], stack[m]).astype(BF16)
            side[m, :, :n] = a[:n]
            side[m, :, n:] = a[n:]
        for m in range(modes):
            wide[m] = dot(side[m], inverse[...])

        pltpu.make_async_copy(amp_own.at[0], amp, arrived).wait()

        def make_d(at):
            rows, low = pl.ds(at, 16), pl.ds(pl.multiple_of(at + n, 16), 16)
            total = jnp.zeros((16, n), F32)
            for m in range(modes):
                fr, fi = wide[m, rows, :n], wide[m, rows, n:]
                total += fr * fr + fi * fi
            factor = amp[rows, :].astype(F32) / jnp.sqrt(total + 1.0) - 1.0
            for m in range(modes):
                stack[m, rows, :] = (wide[m, rows, :n] * factor).astype(BF16)
                stack[m, low, :] = (wide[m, rows, n:] * factor).astype(BF16)
        rows_loop(n, 16, make_d, unroll=True)

        for m in range(modes):
            b = dot(inverse[...], stack[m]).astype(BF16)
            side[m, :, :n] = b[:n]
            side[m, :, n:] = b[n:]
        for m in range(modes):
            wide[m] = dot(side[m], forward[...])

        def finish(at):
            rows = pl.ds(at, 16)
            xr, xi = patch[0, rows, :], patch[1, rows, :]
            tr = jnp.zeros((16, n), F32)
            ti = jnp.zeros((16, n), F32)
            for m in range(modes):
                er, ei = wide[m, rows, :n], wide[m, rows, n:]
                pr = probe[0, m, rows, :].astype(F32)
                pi = probe[1, m, rows, :].astype(F32)
                tr += pr * er + pi * ei
                ti += pr * ei - pi * er
                prb_out[0, m, rows, :] += xr * er + xi * ei
                prb_out[1, m, rows, :] += xr * ei - xi * er
            below = pl.ds(pl.multiple_of(at + 8, 8), 16)
            term[0, below, :] = tr
            term[1, below, :] = ti
        rows_loop(n, 16, finish, unroll=True)

        def paste(at):
            rows = pl.ds(pl.multiple_of(base + at, 8), 24)
            for p in range(2):
                turned = []
                for j in range(inner):
                    x = term[p, pl.ds(at, 32), j * lane:(j + 1) * lane].reshape(4, 8, lane)
                    x = pltpu.roll(x, lax.rem(down, 8), 1)
                    x = jnp.where(out_rows, x[1:], x[:3]).reshape(24, lane)
                    turned.append(pltpu.roll(x, right, 1).reshape(3, 8, lane))
                for j in range(inner + 1):
                    low = turned[j] if j < inner else jnp.zeros((3, 8, lane), F32)
                    high = turned[j - 1] if j > 0 else jnp.zeros((3, 8, lane), F32)
                    grad_out[block + j, p, rows, :] += jnp.where(out_lanes, low, high).reshape(24, lane)
        rows_loop(n + 8, 24, paste, unroll=True)

    slots = KEEP + amp_got.shape[0]

    def item_trip(item, carry):
        own = item < KEEP
        other = jnp.maximum(item - KEEP, 0)
        r = jnp.where(own, rows_own[0, item], rows_got[other, 0, item])
        c = jnp.where(own, cols_own[0, item], cols_got[other, 0, item])
        count = jnp.where(own, count_own[0, 0], count_got[other, 0, 0])

        @pl.when(item < count)
        def _():
            @pl.when(own)
            def _():
                pltpu.make_async_copy(amp_own.at[item], amp, arrived).start()

            @pl.when(jnp.logical_not(own))
            def _():
                pltpu.make_async_copy(amp_got.at[other], amp, arrived).start()
            position(r, c)
        return carry
    lax.fori_loop(0, slots, item_trip, 0)

    @pl.when(edge)
    def _():
        def drop(at):
            grad_out[near:, :, pl.ds(at, 16), :] = jnp.zeros((blocks - near, 2, 16, lane), F32)
        rows_loop(height, 16, drop)


def positions(own, got, tile, halo, probe, amp_own, amp_got, table):
    _, modes, n, _ = probe.shape
    height, tw = tile.shape[1:]
    vmem, anywhere = pl.BlockSpec(memory_space=pltpu.VMEM), pl.BlockSpec(memory_space=pl.ANY)
    hbm = pl.BlockSpec(memory_space=pltpu.HBM)
    return pl.pallas_call(
        positions_kernel,
        out_shape=(
            jax.ShapeDtypeStruct((2 * tw // 128, 2, height, 128), F32),
            jax.ShapeDtypeStruct((2, modes, n, n), F32),
        ),
        in_specs=[hbm] * 3 + [anywhere] * 3 + [hbm, anywhere, hbm, hbm, anywhere, hbm],
        out_specs=(vmem, vmem),
        scratch_shapes=[pltpu.SMEM(m.shape, m.dtype) for m in (*own, *got)] + [
            pltpu.VMEM((2 * tw // 128, 2, height, 128), F32),
            pltpu.VMEM(probe.shape, BF16),
            pltpu.VMEM(table.shape, BF16),
            pltpu.VMEM((n, n), BF16),
            pltpu.VMEM((2, n, n), F32),
            pltpu.VMEM((modes, 2 * n, n), BF16),
            pltpu.VMEM((modes, n, 2 * n), BF16),
            pltpu.VMEM((modes, n, 2 * n), F32),
            pltpu.VMEM((2, n + 16, n), F32),
            pltpu.VMEM((2 * n, 2 * n), BF16),
            pltpu.VMEM((2 * n, 2 * n), BF16),
            pltpu.SemaphoreType.DMA,
            pltpu.SemaphoreType.DMA((8 + 2 * tw // 128,)),
        ],
        compiler_params=pltpu.CompilerParams(vmem_limit_bytes=60 * 1024 * 1024),
        name="positions",
    )(*own, *got, tile, halo, probe, amp_own, amp_got, table)


class Place:
    def __init__(self, sizes):
        self.nz, self.nlo, self.nc, self.nx, self.nhi = sizes
        self.ny = self.nlo * self.nhi
        self.tiles, self.scans = self.nz * self.nlo * self.nc, self.nx * self.nhi
        self.t, self.s = lax.axis_index("tile"), lax.axis_index("scan")
        self.core = lax.rem(self.t, self.nc)
        self.lo = lax.rem(self.t // self.nc, self.nlo)
        self.z = self.t // (self.nc * self.nlo)
        self.x, self.hi = self.s // self.nhi, lax.rem(self.s, self.nhi)
        self.y = self.hi * self.nlo + self.lo

    def device(self, z, y, core, x):
        lo, hi = lax.rem(y, self.nlo), y // self.nlo
        return {"tile": (z * self.nlo + lo) * self.nc + core, "scan": x * self.nhi + hi}

    def along_z(self, d):
        at = lax.rem(self.z + d, self.nz)
        return at, self.device(at, self.y, self.core, self.x)

    def along_y(self, d):
        at = lax.rem(self.y + d, self.ny)
        return at, self.device(self.z, at, self.core, self.x)

    def along_hi(self, d):
        at = lax.rem(self.hi + d, self.nhi)
        return at, self.device(self.z, at * self.nlo + self.lo, self.core, self.x)

    def along_x(self, d):
        at = lax.rem(self.x + d, self.nx)
        return at, self.device(self.z, self.y, self.core, at)

    def tile(self, d):
        return {"tile": lax.rem(self.t + self.tiles + d, self.tiles), "scan": self.s}

    def partner(self):
        return self.device(self.z, self.y, 1 - self.core, self.x)


def greet(devices):
    barrier = pltpu.get_barrier_semaphore()
    for device in devices:
        pl.semaphore_signal(barrier, inc=1, device_id=device, device_id_type=MESH)
    pl.semaphore_wait(barrier, len(devices))


def cube(index):
    high, odd = index // 2, lax.rem(index, 2)
    return ((lax.rem(high + odd, 2), index + 1 - 2 * odd), (high, 3 - index))


def sums_kernel(sizes, object_scale, probe_scaling, grad_in, prb_in, upd_low, upd_high, prb_out,
                grad, prb,
                near1, kept1, near2, kept2, near3, kept3, near4, kept4, shifted,
                give, got, mixed, first, held, second, small, third,
                send, recv, loaded):
    at = Place(sizes)
    used = [0]
    started = []
    middle = prb_in.shape[0] // 2
    theirs = pl.ds(pl.multiple_of((1 - at.core) * middle, 8), middle)
    ours = pl.ds(pl.multiple_of(at.core * middle, 8), middle)
    loads = [
        pltpu.make_async_copy(prb_in.at[theirs, :], prb.at[theirs, :], loaded.at[0]),
        pltpu.make_async_copy(grad_in, grad, loaded.at[1]),
        pltpu.make_async_copy(prb_in.at[ours, :], prb.at[ours, :], loaded.at[2]),
    ]
    for load in loads:
        load.start()

    def copy(src, dst, device):
        k = used[0]
        used[0] += 1
        c = pltpu.make_async_remote_copy(
            src_ref=src, dst_ref=dst, send_sem=send.at[k], recv_sem=recv.at[k],
            device_id=device, device_id_type=MESH)
        c.start()
        started.append(c)
        return c

    greet([at.partner(), at.tile(1), at.tile(-1)]
          + [at.along_z(d)[1] for d in range(1, at.nz)]
          + [at.along_y(d)[1] for d in range(1, at.ny)]
          + [at.along_x(d)[1] for d in range(1, at.nx)])

    height = grad.shape[1]
    total = prb.shape[0]
    half = total // 2
    quart = half // 2

    bits = []
    for h in range(2):
        xb = [(b, at.device(at.z, at.y, at.core, to)) for b, to in cube(at.x)]
        yb = [(b, at.device(at.z, to * at.nlo + at.lo, at.core, at.x)) for b, to in cube(at.hi)]
        bits.append((xb if h == 0 else xb[::-1]) + (yb if h == 0 else yb[::-1]))
    cut = [height // 4, height // 8, height // 16, height // 32]
    near = [near1, near2, near3, near4]
    kept = [kept1, kept2, kept3, kept4]

    def object_source(side, h, stage):
        if stage == 0:
            return grad.at[side], h * (height // 2)
        return kept[stage - 1].at[h, side], 0

    def object_send(side, stage):
        out = []
        for h in range(2):
            bit, device = bits[h][stage]
            src, base = (grad_in.at[side], h * (height // 2)) if stage == 0 else object_source(side, h, stage)
            rows = pl.ds(pl.multiple_of(base + (1 - bit) * cut[stage], 8), cut[stage])
            out.append(copy(src.at[rows, :], near[stage].at[h, side], device))
        return out

    def object_add(side, stage, copies):
        for h in range(2):
            copies[h].wait_recv()
            bit, _ = bits[h][stage]
            src, base = object_source(side, h, stage)
            mine = base + bit * cut[stage]

            def add(r, h=h, src=src, mine=mine):
                rows = pl.ds(r, 48)
                kept[stage][h, side, rows, :] = (
                    src[pl.ds(pl.multiple_of(mine + r, 8), 48), :] + near[stage][h, side, rows, :])
            rows_loop(cut[stage], 48, add, unroll=True)

    upd_out = (upd_low, upd_high)

    def object_place(h, stages):
        base = 0
        for stage in range(stages):
            base += bits[h][stage][0] * cut[stage]
        return base

    def object_gather(stage):
        out = []
        for h in range(2):
            rows = pl.ds(pl.multiple_of(object_place(h, stage + 1), 8), cut[stage])
            out.append(copy(upd_out[h].at[rows, :], upd_out[h].at[rows, :], bits[h][stage][1]))
        return out

    crossing = []

    def objects(side):
        o = object_send(side, 0)
        for stage in range(3):
            yield
            if stage == 0 and side == 1:
                loads[1].wait()
            object_add(side, stage, o)
            o = object_send(side, stage + 1)
        yield
        object_add(side, 3, o)
        if side == 1:
            crossing.append(copy(kept4.at[:, 1], shifted, at.tile(1)))
            return
        yield
        crossing[0].wait_recv()
        for h in range(2):
            place = object_place(h, 4)

            def finish(r, h=h, place=place):
                rows = pl.ds(r, 48)
                upd_out[h][pl.ds(pl.multiple_of(place + r, 8), 48), :] = object_scale * (
                    kept4[h, 0, rows, :] + shifted[h, rows, :])
            rows_loop(cut[3], 48, finish)
        for stage in (3, 2, 1, 0):
            o = object_gather(stage)
            yield
            for c in o:
                c.wait_recv()

    axes = ((at.along_z, at.along_y, at.nz, at.ny, at.z, at.y),
            (at.along_y, at.along_z, at.ny, at.nz, at.y, at.z))

    def far_first(n):
        return sorted(range(1, n), key=lambda d: (-min(d, n - d), d))

    def share(h, origin, device, part=None):
        n1 = axes[h][2]
        size = quart // n1
        base = my_base + h * quart + lax.rem(origin + n1, n1) * size
        if part is not None:
            size = size // 2
            base += part * size
        rows = pl.ds(pl.multiple_of(base, 8), size)
        return copy(prb_out.at[rows, :], prb_out.at[rows, :], device)

    other_base = (1 - at.core) * half
    my_base = at.core * half
    sub = quart // (at.nz * at.ny)

    def probes():
        loads[0].wait()

        def cast_half(r):
            give[pl.ds(r, 32), :] = prb[pl.ds(pl.multiple_of(other_base + r, 8), 32), :].astype(BF16)
        rows_loop(half, 32, cast_half, unroll=4)
        p0 = copy(give, got, at.partner())
        yield
        loads[2].wait()
        p0.wait_recv()

        def mix(r):
            rows = pl.ds(r, 32)
            mine = prb[pl.ds(pl.multiple_of(my_base + r, 8), 32), :]
            mixed[rows, :] = (mine + got[rows, :].astype(F32)).astype(BF16)
        rows_loop(half, 32, mix, unroll=4)
        p1 = [[], []]
        for h, (one, _, n1, n2, c1, c2) in enumerate(axes):
            for d in far_first(n1):
                to, device = one(d)
                rows = quart // n1
                src = mixed.at[pl.ds(pl.multiple_of(h * quart + to * rows, 16), rows), :]
                p1[h].append(copy(src, first.at[h, d - 1, pl.ds(0, rows), :], device))
        yield
        p2 = [[], []]
        for h, (_, two, n1, n2, c1, c2) in enumerate(axes):
            rows = quart // n1
            for c in p1[h]:
                c.wait_recv()
            base = h * quart + c1 * rows

            def add_first(r, h=h, n1=n1, base=base):
                acc = (prb[pl.ds(pl.multiple_of(my_base + base + r, 8), 16), :]
                       + got[pl.ds(pl.multiple_of(base + r, 16), 16), :].astype(F32))
                for d in range(n1 - 1):
                    acc += first[h, d, pl.ds(r, 16), :].astype(F32)
                held[h, pl.ds(r, 16), :] = acc
            rows_loop(rows, 16, add_first, unroll=True)
            for d in far_first(n2):
                to, device = two(d)
                src = held.at[h, pl.ds(pl.multiple_of(to * sub, 8), sub), :]
                p2[h].append(copy(src, second.at[h, d - 1], device))
        yield
        for h, (_, _, n1, n2, c1, c2) in enumerate(axes):
            for c in p2[h]:
                c.wait_recv()
            acc = held[h, pl.ds(pl.multiple_of(c2 * sub, 8), sub), :]
            for d in range(n2 - 1):
                acc += second[h, d]
            small[h] = acc
            third[at.x, h] = acc
        p3 = [copy(small, third.at[at.x], at.along_x(d)[1]) for d in far_first(at.nx)]
        yield
        for c in p3:
            c.wait_recv()
        p4 = [[], []]
        for h, (_, two, n1, n2, c1, c2) in enumerate(axes):
            acc = third[0, h]
            for k in range(1, at.nx):
                acc += third[k, h]
            rows = pl.ds(pl.multiple_of(my_base + h * quart + c1 * (quart // n1) + c2 * sub, 8), sub)
            prb_out[rows, :] = probe_scaling * acc
            for d in far_first(n2):
                p4[h].append(copy(prb_out.at[rows, :], prb_out.at[rows, :], two(d)[1]))
        yield
        for h in range(2):
            for c in p4[h]:
                c.wait_recv()
        p6 = []
        steps = max(at.nz, at.ny) // 2

        def ring_send(k, part):
            out = {}
            for h, (one, _, n1, _, c1, _) in enumerate(axes):
                for side in range(2):
                    if 2 * k < n1 or (2 * k == n1 and side == part):
                        ahead = one(1 if side == 0 else n1 - 1)[1]
                        out[h, side] = share(h, c1 - (k - 1) if side == 0 else c1 + (k - 1), ahead, part)
            return out

        ring = [ring_send(1, part) for part in range(2)]
        for h in range(2):
            p6.append(share(h, axes[h][4], at.partner()))
        for k in range(1, steps + 1):
            for part in range(2):
                yield
                for c in ring[part].values():
                    c.wait_recv()
                passed = ring[part]
                ring[part] = ring_send(k + 1, part) if k < steps else {}
                for h, side in passed:
                    p6.append(share(h, axes[h][4] - k if side == 0 else axes[h][4] + k, at.partner(), part))
        yield
        for c in p6:
            c.wait_recv()

    chains = {"r": objects(1), "l": objects(0), "p": probes()}
    for turn in ORDER:
        next(chains[turn], None)
    for c in started:
        c.wait_send()


def sums(sizes, grad, prb, object_scale=1.0, probe_scaling=1.0):
    nz, nlo, nc, nx, nhi = sizes
    ny = nlo * nhi
    height, width = grad.shape[1:]
    total, pw = prb.shape
    half, quart = total // 2, total // 4
    long, short = max(nz, ny), min(nz, ny)
    sub = quart // (nz * ny)
    vmem = pl.BlockSpec(memory_space=pltpu.VMEM)
    stages = []
    for k in (4, 8, 16, 32):
        stages += [pltpu.VMEM((2, 2, height // k, width), F32)] * 2
    return pl.pallas_call(
        functools.partial(sums_kernel, sizes, object_scale, probe_scaling),
        out_shape=(
            jax.ShapeDtypeStruct((height // 2, width), F32),
            jax.ShapeDtypeStruct((height // 2, width), F32),
            jax.ShapeDtypeStruct((total, pw), F32),
        ),
        in_specs=[pl.BlockSpec(memory_space=pl.ANY)] * 2,
        out_specs=(vmem, vmem, vmem),
        scratch_shapes=[pltpu.VMEM(grad.shape, F32), pltpu.VMEM(prb.shape, F32)] + stages + [
            pltpu.VMEM((2, height // 32, width), F32),
            pltpu.VMEM((half, pw), BF16),
            pltpu.VMEM((half, pw), BF16),
            pltpu.VMEM((half, pw), BF16),
            pltpu.VMEM((2, long - 1, quart // short, pw), BF16),
            pltpu.VMEM((2, quart // short, pw), F32),
            pltpu.VMEM((2, long - 1, sub, pw), F32),
            pltpu.VMEM((2, sub, pw), F32),
            pltpu.VMEM((nx, 2, sub, pw), F32),
            pltpu.SemaphoreType.DMA((COPIES,)),
            pltpu.SemaphoreType.DMA((COPIES,)),
            pltpu.SemaphoreType.DMA((3,)),
        ],
        compiler_params=pltpu.CompilerParams(
            collective_id=1, has_side_effects=True, vmem_limit_bytes=52 << 20),
        name="sums",
    )(grad, prb)


def spread_kernel(sizes, tile, amp, rows, cols, count, halo, amp_got, rows_got, cols_got, count_got, send, recv):
    at = Place(sizes)
    moved = amp_got.shape[0]
    keep = amp.shape[0] - moved
    devices = [at.along_x(d)[1] for d in range(1, moved + 1)]
    greet([at.tile(1), at.tile(-1)] + devices)
    copies = []

    def copy(src, dst, device):
        k = len(copies)
        c = pltpu.make_async_remote_copy(
            src_ref=src, dst_ref=dst, send_sem=send.at[k], recv_sem=recv.at[k],
            device_id=device, device_id_type=MESH)
        c.start()
        copies.append(c)

    copy(tile, halo, at.tile(-1))
    for k, device in enumerate(devices):
        copy(amp.at[keep + k], amp_got.at[k], device)
        copy(rows, rows_got.at[k], device)
        copy(cols, cols_got.at[k], device)
        copy(count, count_got.at[k], device)
    for c in copies:
        c.wait()


def spread(sizes, moved, tile, amp, *meta):
    anywhere = pl.BlockSpec(memory_space=pl.ANY)
    copies = 1 + (1 + len(meta)) * moved
    return pl.pallas_call(
        functools.partial(spread_kernel, sizes),
        out_shape=(
            jax.ShapeDtypeStruct(tile.shape, tile.dtype),
            jax.ShapeDtypeStruct((moved,) + amp.shape[1:], amp.dtype),
        ) + tuple(jax.ShapeDtypeStruct((moved,) + m.shape, m.dtype) for m in meta),
        in_specs=[pl.BlockSpec(memory_space=pltpu.HBM)] * (2 + len(meta)),
        out_specs=(anywhere,) * (2 + len(meta)),
        scratch_shapes=[pltpu.SemaphoreType.DMA((copies,))] * 2,
        compiler_params=pltpu.CompilerParams(
            collective_id=0, has_side_effects=True, vmem_limit_bytes=60 * 1024 * 1024),
        name="spread",
    )(tile, amp, *meta)


def on_device(object_tiles, probe_modes, amplitudes, row_offsets, col_offsets, slot_counts):
    slots = amplitudes.shape[2]
    meta = (row_offsets[0], col_offsets[0], slot_counts)
    halo, amp_got, *meta_got = spread(SIZES, slots - KEEP, object_tiles, amplitudes[0, 0], *meta)
    grad, probe_grad = positions(
        meta, meta_got, object_tiles, halo, probe_modes, amplitudes[0, 0], amp_got,
        dft_tables(probe_modes.shape[2]),
    )
    factor = probe_scale / math.sqrt(lax.axis_size("tile") * lax.axis_size("scan"))
    blocks, _, height, lane = grad.shape
    *update, change = sums(
        SIZES, grad.reshape(2, -1, lane), probe_grad.reshape(-1, probe_modes.shape[3]), object_step, factor)
    update = jnp.concatenate([u.reshape(2, height, lane) for u in update], axis=2)
    new_object = object_tiles + update
    new_probe = probe_modes.astype(F32) + change.reshape(probe_modes.shape)
    return (new_object, new_probe)


def solution(mesh):
    nz, nlo, nc, nx, nhi = SIZES
    if mesh.shape["tile"] != nz * nlo * nc or mesh.shape["scan"] != nx * nhi:
        raise ValueError("other mesh")
    placed = (
        P(None, None, "tile"),
        P(),
        P("tile", "scan", None, None, None),
        P("tile", "scan", None),
        P("tile", "scan", None),
        P("tile", "scan"),
    )
    return jax.shard_map(
        on_device,
        mesh=mesh,
        in_specs=placed,
        out_specs=(P(None, None, "tile"), P()),
        check_vma=False,
    )
```

```python
import functools
import math

import jax
import jax.numpy as jnp
import numpy as np
from jax import lax
from jax.experimental import pallas as pl
from jax.experimental.pallas import tpu as pltpu
from jax.sharding import PartitionSpec as P

F32, BF16 = jnp.float32, jnp.bfloat16
MESH = pl.DeviceIdType.MESH
KEEP = 2
COPIES = 136
ORDER = "rlpprlprlprlrlplrplpplpplpplpplpllpppppppllllllllll"
SIZES = (8, 2, 2, 4, 4)
object_step = 0.1
probe_scale = 0.5


def dft_tables(extent):
    index = np.arange(extent)
    angle = (index[:, None] * index[None, :] % extent) * (2.0 * math.pi / extent)
    factor = 1.0 / math.sqrt(extent)
    table = np.stack([np.cos(angle) * factor, -np.sin(angle) * factor])
    return jnp.asarray(table.astype(np.float32)).astype(BF16)


def rows_loop(total, step, body, unroll=1):
    def trip(i, carry):
        body(pl.multiple_of(i * step, step))
        return carry
    lax.fori_loop(0, total // step, trip, 0, unroll=unroll)


def dot(a, b):
    return jnp.dot(a, b, preferred_element_type=F32)


def positions_kernel(rows_own_in, cols_own_in, count_own_in, rows_got_in, cols_got_in, count_got_in,
                     tile_in, halo_in, probe_in, amp_own, amp_got, table_in,
                     grad_out, prb_out,
                     rows_own, cols_own, count_own, rows_got, cols_got, count_got, ext, probe, table,
                     amp, patch, stack, side, wide, term, forward, inverse, arrived, loaded):
    n = probe.shape[2]
    modes = probe.shape[1]
    blocks, _, height, lane = grad_out.shape
    near, inner = blocks // 2, n // lane
    moves = [(tile_in.at[:, :, pl.ds(b * lane, lane)], ext.at[b]) for b in range(near)]
    moves += [(halo_in.at[:, :, pl.ds(b * lane, lane)], ext.at[near + b]) for b in range(near)]
    moves += [
        (probe_in, probe), (table_in, table),
        (rows_own_in, rows_own), (cols_own_in, cols_own), (count_own_in, count_own),
        (rows_got_in, rows_got), (cols_got_in, cols_got), (count_got_in, count_got),
    ]
    loads = [pltpu.make_async_copy(src, dst, loaded.at[k]) for k, (src, dst) in enumerate(moves)]
    for load in loads:
        load.start()
    edge = lax.axis_index("tile") == lax.axis_size("tile") - 1

    def clear(at):
        grad_out[:, :, pl.ds(at, 16), :] = jnp.zeros((blocks, 2, 16, lane), F32)
    rows_loop(height, 16, clear)

    def clear_probe(at):
        prb_out[:, :, pl.ds(at, 16), :] = jnp.zeros((2, modes, 16, n), F32)
    rows_loop(n, 16, clear_probe)
    term[:, :8, :] = jnp.zeros((2, 8, n), F32)
    term[:, n + 8:, :] = jnp.zeros((2, 8, n), F32)
    for load in loads:
        load.wait()

    @pl.when(edge)
    def _():
        def drop(at):
            ext[near:, :, pl.ds(at, 16), :] = jnp.zeros((blocks - near, 2, 16, lane), F32)
        rows_loop(height, 16, drop)
    forward[:n, :n] = table[0]
    forward[n:, n:] = table[0]
    forward[n:, :n] = table[1]
    forward[:n, n:] = -table[1]
    inverse[:n, :n] = table[0]
    inverse[n:, n:] = table[0]
    inverse[n:, :n] = -table[1]
    inverse[:n, n:] = table[1]

    def position(r, c):
        base = pl.multiple_of(jnp.minimum(r // 8 * 8, height - n - 8), 8)
        down = r - base
        block, right = c // lane, lax.rem(c, lane)
        up, left = lax.rem(8 - down, 8), lax.rem(lane - right, lane)
        lanes = lax.broadcasted_iota(jnp.int32, (8, lane), 1)
        rows8 = lax.broadcasted_iota(jnp.int32, (8, lane), 0)
        in_lanes, in_rows = lanes < lane - right, rows8 < 8 - down
        out_lanes, out_rows = lanes >= right, rows8 >= down

        def cut(at):
            for p in range(2):
                turned = [
                    pltpu.roll(ext[block + j, p, pl.ds(pl.multiple_of(base + at, 8), 40), :], left, 1).reshape(5, 8, lane)
                    for j in range(inner + 1)
                ]
                for j in range(inner):
                    x = jnp.where(in_lanes, turned[j], turned[j + 1])
                    x = pltpu.roll(x, up, 1)
                    x = jnp.where(in_rows, x[:4], x[1:])
                    patch[p, pl.ds(at, 32), j * lane:(j + 1) * lane] = x.reshape(32, lane)
        rows_loop(n, 32, cut, unroll=True)

        def make_psi(at):
            rows, low = pl.ds(at, 16), pl.ds(pl.multiple_of(at + n, 16), 16)
            xr, xi = patch[0, rows, :], patch[1, rows, :]
            for m in range(modes):
                pr = probe[0, m, rows, :].astype(F32)
                pi = probe[1, m, rows, :].astype(F32)
                stack[m, rows, :] = (pr * xr - pi * xi).astype(BF16)
                stack[m, low, :] = (pr * xi + pi * xr).astype(BF16)
        rows_loop(n, 16, make_psi, unroll=True)

        for m in range(modes):
            a = dot(forward[...], stack[m]).astype(BF16)
            side[m, :, :n] = a[:n]
            side[m, :, n:] = a[n:]
        for m in range(modes):
            wide[m] = dot(side[m], inverse[...])

        pltpu.make_async_copy(amp_own.at[0], amp, arrived).wait()

        def make_d(at):
            rows, low = pl.ds(at, 16), pl.ds(pl.multiple_of(at + n, 16), 16)
            total = jnp.zeros((16, n), F32)
            for m in range(modes):
                fr, fi = wide[m, rows, :n], wide[m, rows, n:]
                total += fr * fr + fi * fi
            factor = amp[rows, :].astype(F32) / jnp.sqrt(total + 1.0) - 1.0
            for m in range(modes):
                stack[m, rows, :] = (wide[m, rows, :n] * factor).astype(BF16)
                stack[m, low, :] = (wide[m, rows, n:] * factor).astype(BF16)
        rows_loop(n, 16, make_d, unroll=True)

        for m in range(modes):
            b = dot(inverse[...], stack[m]).astype(BF16)
            side[m, :, :n] = b[:n]
            side[m, :, n:] = b[n:]
        for m in range(modes):
            wide[m] = dot(side[m], forward[...])

        def finish(at):
            rows = pl.ds(at, 16)
            xr, xi = patch[0, rows, :], patch[1, rows, :]
            tr = jnp.zeros((16, n), F32)
            ti = jnp.zeros((16, n), F32)
            for m in range(modes):
                er, ei = wide[m, rows, :n], wide[m, rows, n:]
                pr = probe[0, m, rows, :].astype(F32)
                pi = probe[1, m, rows, :].astype(F32)
                tr += pr * er + pi * ei
                ti += pr * ei - pi * er
                prb_out[0, m, rows, :] += xr * er + xi * ei
                prb_out[1, m, rows, :] += xr * ei - xi * er
            below = pl.ds(pl.multiple_of(at + 8, 8), 16)
            term[0, below, :] = tr
            term[1, below, :] = ti
        rows_loop(n, 16, finish, unroll=True)

        def paste(at):
            rows = pl.ds(pl.multiple_of(base + at, 8), 24)
            for p in range(2):
                turned = []
                for j in range(inner):
                    x = term[p, pl.ds(at, 32), j * lane:(j + 1) * lane].reshape(4, 8, lane)
                    x = pltpu.roll(x, lax.rem(down, 8), 1)
                    x = jnp.where(out_rows, x[1:], x[:3]).reshape(24, lane)
                    turned.append(pltpu.roll(x, right, 1).reshape(3, 8, lane))
                for j in range(inner + 1):
                    low = turned[j] if j < inner else jnp.zeros((3, 8, lane), F32)
                    high = turned[j - 1] if j > 0 else jnp.zeros((3, 8, lane), F32)
                    grad_out[block + j, p, rows, :] += jnp.where(out_lanes, low, high).reshape(24, lane)
        rows_loop(n + 8, 24, paste, unroll=True)

    slots = KEEP + amp_got.shape[0]

    def item_trip(item, carry):
        own = item < KEEP
        other = jnp.maximum(item - KEEP, 0)
        r = jnp.where(own, rows_own[0, item], rows_got[other, 0, item])
        c = jnp.where(own, cols_own[0, item], cols_got[other, 0, item])
        count = jnp.where(own, count_own[0, 0], count_got[other, 0, 0])

        @pl.when(item < count)
        def _():
            @pl.when(own)
            def _():
                pltpu.make_async_copy(amp_own.at[item], amp, arrived).start()

            @pl.when(jnp.logical_not(own))
            def _():
                pltpu.make_async_copy(amp_got.at[other], amp, arrived).start()
            position(r, c)
        return carry
    lax.fori_loop(0, slots, item_trip, 0)

    @pl.when(edge)
    def _():
        def drop(at):
            grad_out[near:, :, pl.ds(at, 16), :] = jnp.zeros((blocks - near, 2, 16, lane), F32)
        rows_loop(height, 16, drop)


def positions(own, got, tile, halo, probe, amp_own, amp_got, table):
    _, modes, n, _ = probe.shape
    height, tw = tile.shape[1:]
    vmem, anywhere = pl.BlockSpec(memory_space=pltpu.VMEM), pl.BlockSpec(memory_space=pl.ANY)
    hbm = pl.BlockSpec(memory_space=pltpu.HBM)
    return pl.pallas_call(
        positions_kernel,
        out_shape=(
            jax.ShapeDtypeStruct((2 * tw // 128, 2, height, 128), F32),
            jax.ShapeDtypeStruct((2, modes, n, n), F32),
        ),
        in_specs=[hbm] * 3 + [anywhere] * 3 + [hbm, anywhere, hbm, hbm, anywhere, hbm],
        out_specs=(vmem, vmem),
        scratch_shapes=[pltpu.SMEM(m.shape, m.dtype) for m in (*own, *got)] + [
            pltpu.VMEM((2 * tw // 128, 2, height, 128), F32),
            pltpu.VMEM(probe.shape, BF16),
            pltpu.VMEM(table.shape, BF16),
            pltpu.VMEM((n, n), BF16),
            pltpu.VMEM((2, n, n), F32),
            pltpu.VMEM((modes, 2 * n, n), BF16),
            pltpu.VMEM((modes, n, 2 * n), BF16),
            pltpu.VMEM((modes, n, 2 * n), F32),
            pltpu.VMEM((2, n + 16, n), F32),
            pltpu.VMEM((2 * n, 2 * n), BF16),
            pltpu.VMEM((2 * n, 2 * n), BF16),
            pltpu.SemaphoreType.DMA,
            pltpu.SemaphoreType.DMA((8 + 2 * tw // 128,)),
        ],
        compiler_params=pltpu.CompilerParams(vmem_limit_bytes=60 * 1024 * 1024),
        name="positions",
    )(*own, *got, tile, halo, probe, amp_own, amp_got, table)


class Place:
    def __init__(self, sizes):
        self.nz, self.nlo, self.nc, self.nx, self.nhi = sizes
        self.ny = self.nlo * self.nhi
        self.tiles, self.scans = self.nz * self.nlo * self.nc, self.nx * self.nhi
        self.t, self.s = lax.axis_index("tile"), lax.axis_index("scan")
        self.core = lax.rem(self.t, self.nc)
        self.lo = lax.rem(self.t // self.nc, self.nlo)
        self.z = self.t // (self.nc * self.nlo)
        self.x, self.hi = self.s // self.nhi, lax.rem(self.s, self.nhi)
        self.y = self.hi * self.nlo + self.lo

    def device(self, z, y, core, x):
        lo, hi = lax.rem(y, self.nlo), y // self.nlo
        return {"tile": (z * self.nlo + lo) * self.nc + core, "scan": x * self.nhi + hi}

    def along_z(self, d):
        at = lax.rem(self.z + d, self.nz)
        return at, self.device(at, self.y, self.core, self.x)

    def along_y(self, d):
        at = lax.rem(self.y + d, self.ny)
        return at, self.device(self.z, at, self.core, self.x)

    def along_hi(self, d):
        at = lax.rem(self.hi + d, self.nhi)
        return at, self.device(self.z, at * self.nlo + self.lo, self.core, self.x)

    def along_x(self, d):
        at = lax.rem(self.x + d, self.nx)
        return at, self.device(self.z, self.y, self.core, at)

    def tile(self, d):
        return {"tile": lax.rem(self.t + self.tiles + d, self.tiles), "scan": self.s}

    def partner(self):
        return self.device(self.z, self.y, 1 - self.core, self.x)


def greet(devices):
    barrier = pltpu.get_barrier_semaphore()
    for device in devices:
        pl.semaphore_signal(barrier, inc=1, device_id=device, device_id_type=MESH)
    pl.semaphore_wait(barrier, len(devices))


def cube(index):
    high, odd = index // 2, lax.rem(index, 2)
    return ((lax.rem(high + odd, 2), index + 1 - 2 * odd), (high, 3 - index))


def sums_kernel(sizes, object_scale, probe_scaling, grad, prb, upd_low, upd_high, prb_out,
                near1, kept1, near2, kept2, near3, kept3, near4, kept4, shifted,
                give, got, mixed, first, held, second, small, third,
                send, recv):
    at = Place(sizes)
    used = [0]
    started = []

    def copy(src, dst, device):
        k = used[0]
        used[0] += 1
        c = pltpu.make_async_remote_copy(
            src_ref=src, dst_ref=dst, send_sem=send.at[k], recv_sem=recv.at[k],
            device_id=device, device_id_type=MESH)
        c.start()
        started.append(c)
        return c

    greet([at.partner(), at.tile(1), at.tile(-1)]
          + [at.along_z(d)[1] for d in range(1, at.nz)]
          + [at.along_y(d)[1] for d in range(1, at.ny)]
          + [at.along_x(d)[1] for d in range(1, at.nx)])

    height = grad.shape[1]
    total = prb.shape[0]
    half = total // 2
    quart = half // 2

    bits = []
    for h in range(2):
        xb = [(b, at.device(at.z, at.y, at.core, to)) for b, to in cube(at.x)]
        yb = [(b, at.device(at.z, to * at.nlo + at.lo, at.core, at.x)) for b, to in cube(at.hi)]
        bits.append((xb if h == 0 else xb[::-1]) + (yb if h == 0 else yb[::-1]))
    cut = [height // 4, height // 8, height // 16, height // 32]
    near = [near1, near2, near3, near4]
    kept = [kept1, kept2, kept3, kept4]

    def object_source(side, h, stage):
        if stage == 0:
            return grad.at[side], h * (height // 2)
        return kept[stage - 1].at[h, side], 0

    def object_send(side, stage):
        out = []
        for h in range(2):
            bit, device = bits[h][stage]
            src, base = object_source(side, h, stage)
            rows = pl.ds(pl.multiple_of(base + (1 - bit) * cut[stage], 8), cut[stage])
            out.append(copy(src.at[rows, :], near[stage].at[h, side], device))
        return out

    def object_add(side, stage, copies):
        for h in range(2):
            copies[h].wait_recv()
            bit, _ = bits[h][stage]
            src, base = object_source(side, h, stage)
            mine = base + bit * cut[stage]

            def add(r, h=h, src=src, mine=mine):
                rows = pl.ds(r, 48)
                kept[stage][h, side, rows, :] = (
                    src[pl.ds(pl.multiple_of(mine + r, 8), 48), :] + near[stage][h, side, rows, :])
            rows_loop(cut[stage], 48, add, unroll=True)

    upd_out = (upd_low, upd_high)

    def object_place(h, stages):
        base = 0
        for stage in range(stages):
            base += bits[h][stage][0] * cut[stage]
        return base

    def object_gather(stage):
        out = []
        for h in range(2):
            rows = pl.ds(pl.multiple_of(object_place(h, stage + 1), 8), cut[stage])
            out.append(copy(upd_out[h].at[rows, :], upd_out[h].at[rows, :], bits[h][stage][1]))
        return out

    crossing = []

    def objects(side):
        o = object_send(side, 0)
        for stage in range(3):
            yield
            object_add(side, stage, o)
            o = object_send(side, stage + 1)
        yield
        object_add(side, 3, o)
        if side == 1:
            crossing.append(copy(kept4.at[:, 1], shifted, at.tile(1)))
            return
        yield
        crossing[0].wait_recv()
        for h in range(2):
            place = object_place(h, 4)

            def finish(r, h=h, place=place):
                rows = pl.ds(r, 48)
                upd_out[h][pl.ds(pl.multiple_of(place + r, 8), 48), :] = object_scale * (
                    kept4[h, 0, rows, :] + shifted[h, rows, :])
            rows_loop(cut[3], 48, finish)
        for stage in (3, 2, 1, 0):
            o = object_gather(stage)
            yield
            for c in o:
                c.wait_recv()

    axes = ((at.along_z, at.along_y, at.nz, at.ny, at.z, at.y),
            (at.along_y, at.along_z, at.ny, at.nz, at.y, at.z))

    def far_first(n):
        return sorted(range(1, n), key=lambda d: (-min(d, n - d), d))

    def share(h, origin, device, part=None):
        n1 = axes[h][2]
        size = quart // n1
        base = my_base + h * quart + lax.rem(origin + n1, n1) * size
        if part is not None:
            size = size // 2
            base += part * size
        rows = pl.ds(pl.multiple_of(base, 8), size)
        return copy(prb_out.at[rows, :], prb_out.at[rows, :], device)

    other_base = (1 - at.core) * half
    my_base = at.core * half
    sub = quart // (at.nz * at.ny)

    def probes():
        def cast_half(r):
            give[pl.ds(r, 32), :] = prb[pl.ds(pl.multiple_of(other_base + r, 8), 32), :].astype(BF16)
        rows_loop(half, 32, cast_half, unroll=4)
        p0 = copy(give, got, at.partner())
        yield
        p0.wait_recv()

        def mix(r):
            rows = pl.ds(r, 32)
            mine = prb[pl.ds(pl.multiple_of(my_base + r, 8), 32), :]
            mixed[rows, :] = (mine + got[rows, :].astype(F32)).astype(BF16)
        rows_loop(half, 32, mix, unroll=4)
        p1 = [[], []]
        for h, (one, _, n1, n2, c1, c2) in enumerate(axes):
            for d in far_first(n1):
                to, device = one(d)
                rows = quart // n1
                src = mixed.at[pl.ds(pl.multiple_of(h * quart + to * rows, 16), rows), :]
                p1[h].append(copy(src, first.at[h, d - 1, pl.ds(0, rows), :], device))
        yield
        p2 = [[], []]
        for h, (_, two, n1, n2, c1, c2) in enumerate(axes):
            rows = quart // n1
            for c in p1[h]:
                c.wait_recv()
            base = h * quart + c1 * rows

            def add_first(r, h=h, n1=n1, base=base):
                acc = (prb[pl.ds(pl.multiple_of(my_base + base + r, 8), 16), :]
                       + got[pl.ds(pl.multiple_of(base + r, 16), 16), :].astype(F32))
                for d in range(n1 - 1):
                    acc += first[h, d, pl.ds(r, 16), :].astype(F32)
                held[h, pl.ds(r, 16), :] = acc
            rows_loop(rows, 16, add_first, unroll=True)
            for d in far_first(n2):
                to, device = two(d)
                src = held.at[h, pl.ds(pl.multiple_of(to * sub, 8), sub), :]
                p2[h].append(copy(src, second.at[h, d - 1], device))
        yield
        for h, (_, _, n1, n2, c1, c2) in enumerate(axes):
            for c in p2[h]:
                c.wait_recv()
            acc = held[h, pl.ds(pl.multiple_of(c2 * sub, 8), sub), :]
            for d in range(n2 - 1):
                acc += second[h, d]
            small[h] = acc
            third[at.x, h] = acc
        p3 = [copy(small, third.at[at.x], at.along_x(d)[1]) for d in far_first(at.nx)]
        yield
        for c in p3:
            c.wait_recv()
        p4 = [[], []]
        for h, (_, two, n1, n2, c1, c2) in enumerate(axes):
            acc = third[0, h]
            for k in range(1, at.nx):
                acc += third[k, h]
            rows = pl.ds(pl.multiple_of(my_base + h * quart + c1 * (quart // n1) + c2 * sub, 8), sub)
            prb_out[rows, :] = probe_scaling * acc
            for d in far_first(n2):
                p4[h].append(copy(prb_out.at[rows, :], prb_out.at[rows, :], two(d)[1]))
        yield
        for h in range(2):
            for c in p4[h]:
                c.wait_recv()
        p6 = []
        steps = max(at.nz, at.ny) // 2

        def ring_send(k, part):
            out = {}
            for h, (one, _, n1, _, c1, _) in enumerate(axes):
                for side in range(2):
                    if 2 * k < n1 or (2 * k == n1 and side == part):
                        ahead = one(1 if side == 0 else n1 - 1)[1]
                        out[h, side] = share(h, c1 - (k - 1) if side == 0 else c1 + (k - 1), ahead, part)
            return out

        ring = [ring_send(1, part) for part in range(2)]
        for h in range(2):
            p6.append(share(h, axes[h][4], at.partner()))
        for k in range(1, steps + 1):
            for part in range(2):
                yield
                for c in ring[part].values():
                    c.wait_recv()
                passed = ring[part]
                ring[part] = ring_send(k + 1, part) if k < steps else {}
                for h, side in passed:
                    p6.append(share(h, axes[h][4] - k if side == 0 else axes[h][4] + k, at.partner(), part))
        yield
        for c in p6:
            c.wait_recv()

    chains = {"r": objects(1), "l": objects(0), "p": probes()}
    for turn in ORDER:
        next(chains[turn], None)
    for c in started:
        c.wait_send()


def sums(sizes, grad, prb, object_scale=1.0, probe_scaling=1.0):
    nz, nlo, nc, nx, nhi = sizes
    ny = nlo * nhi
    height, width = grad.shape[1:]
    total, pw = prb.shape
    half, quart = total // 2, total // 4
    long, short = max(nz, ny), min(nz, ny)
    sub = quart // (nz * ny)
    vmem = pl.BlockSpec(memory_space=pltpu.VMEM)
    stages = []
    for k in (4, 8, 16, 32):
        stages += [pltpu.VMEM((2, 2, height // k, width), F32)] * 2
    return pl.pallas_call(
        functools.partial(sums_kernel, sizes, object_scale, probe_scaling),
        out_shape=(
            jax.ShapeDtypeStruct((height // 2, width), F32),
            jax.ShapeDtypeStruct((height // 2, width), F32),
            jax.ShapeDtypeStruct((total, pw), F32),
        ),
        in_specs=[vmem, vmem],
        out_specs=(vmem, vmem, vmem),
        scratch_shapes=stages + [
            pltpu.VMEM((2, height // 32, width), F32),
            pltpu.VMEM((half, pw), BF16),
            pltpu.VMEM((half, pw), BF16),
            pltpu.VMEM((half, pw), BF16),
            pltpu.VMEM((2, long - 1, quart // short, pw), BF16),
            pltpu.VMEM((2, quart // short, pw), F32),
            pltpu.VMEM((2, long - 1, sub, pw), F32),
            pltpu.VMEM((2, sub, pw), F32),
            pltpu.VMEM((nx, 2, sub, pw), F32),
            pltpu.SemaphoreType.DMA((COPIES,)),
            pltpu.SemaphoreType.DMA((COPIES,)),
        ],
        compiler_params=pltpu.CompilerParams(
            collective_id=1, has_side_effects=True, vmem_limit_bytes=40 << 20),
        name="sums",
    )(grad, prb)


def spread_kernel(sizes, tile, amp, rows, cols, count, halo, amp_got, rows_got, cols_got, count_got, send, recv):
    at = Place(sizes)
    moved = amp_got.shape[0]
    keep = amp.shape[0] - moved
    devices = [at.along_x(d)[1] for d in range(1, moved + 1)]
    across = jnp.where(at.lo == 0, at.nhi - 1, 1)
    to_hi = lax.rem(at.hi + jnp.where(at.core == 0, across, 0), at.nhi)
    from_hi = jnp.where(at.core == 1, lax.rem(at.hi + jnp.where(at.lo == 1, 1, at.nhi - 1), at.nhi), at.hi)
    beyond = {"tile": at.tile(-1)["tile"], "scan": at.x * at.nhi + to_hi}
    behind = {"tile": at.tile(1)["tile"], "scan": at.x * at.nhi + from_hi}
    greet([at.tile(1), at.tile(-1), beyond, behind] + devices)
    copies = []

    def copy(src, dst, device):
        k = len(copies)
        c = pltpu.make_async_remote_copy(
            src_ref=src, dst_ref=dst, send_sem=send.at[k], recv_sem=recv.at[k],
            device_id=device, device_id_type=MESH)
        c.start()
        copies.append(c)

    copy(tile.at[0], halo.at[0], at.tile(-1))
    copy(tile.at[1], halo.at[1], beyond)
    for k, device in enumerate(devices):
        copy(amp.at[keep + k], amp_got.at[k], device)
        copy(rows, rows_got.at[k], device)
        copy(cols, cols_got.at[k], device)
        copy(count, count_got.at[k], device)
    for c in copies:
        c.wait()


def spread(sizes, moved, tile, amp, *meta):
    anywhere = pl.BlockSpec(memory_space=pl.ANY)
    copies = 2 + (1 + len(meta)) * moved
    return pl.pallas_call(
        functools.partial(spread_kernel, sizes),
        out_shape=(
            jax.ShapeDtypeStruct(tile.shape, tile.dtype),
            jax.ShapeDtypeStruct((moved,) + amp.shape[1:], amp.dtype),
        ) + tuple(jax.ShapeDtypeStruct((moved,) + m.shape, m.dtype) for m in meta),
        in_specs=[pl.BlockSpec(memory_space=pltpu.HBM)] * (2 + len(meta)),
        out_specs=(anywhere,) * (2 + len(meta)),
        scratch_shapes=[pltpu.SemaphoreType.DMA((copies,))] * 2,
        compiler_params=pltpu.CompilerParams(
            collective_id=0, has_side_effects=True, vmem_limit_bytes=60 * 1024 * 1024),
        name="spread",
    )(tile, amp, *meta)


def on_device(object_tiles, probe_modes, amplitudes, row_offsets, col_offsets, slot_counts):
    slots = amplitudes.shape[2]
    meta = (row_offsets[0], col_offsets[0], slot_counts)
    halo, amp_got, *meta_got = spread(SIZES, slots - KEEP, object_tiles, amplitudes[0, 0], *meta)
    grad, probe_grad = positions(
        meta, meta_got, object_tiles, halo, probe_modes, amplitudes[0, 0], amp_got,
        dft_tables(probe_modes.shape[2]),
    )
    factor = probe_scale / math.sqrt(lax.axis_size("tile") * lax.axis_size("scan"))
    blocks, _, height, lane = grad.shape
    *update, change = sums(
        SIZES, grad.reshape(2, -1, lane), probe_grad.reshape(-1, probe_modes.shape[3]), object_step, factor)
    update = jnp.concatenate([u.reshape(2, height, lane) for u in update], axis=2)
    new_object = object_tiles + update
    new_probe = probe_modes.astype(F32) + change.reshape(probe_modes.shape)
    return (new_object, new_probe)


def solution(mesh):
    nz, nlo, nc, nx, nhi = SIZES
    if mesh.shape["tile"] != nz * nlo * nc or mesh.shape["scan"] != nx * nhi:
        raise ValueError("other mesh")
    placed = (
        P(None, None, "tile"),
        P(),
        P("tile", "scan", None, None, None),
        P("tile", "scan", None),
        P("tile", "scan", None),
        P("tile", "scan"),
    )
    return jax.shard_map(
        on_device,
        mesh=mesh,
        in_specs=placed,
        out_specs=(P(None, None, "tile"), P()),
        check_vma=False,
    )
```
